128 devices in a mesh: theta: 16 (over x, y_hi, core), phi: 8 (over z, y_lo).
Axes of the slice: x: 4, y: 4 (y_hi: 2, y_lo: 2; y = y_hi * 2 + y_lo), z: 4, core: 2. Of those that a mesh axis runs over, the one named last changes fastest.
Arguments:
- child_out: float32 [8, 192, 384, 128], P(None, 'theta', 'phi'), may hold values from -6 to 6
- child_slot: int32 [128], replicated, may hold values from 0 to 127, each once
- sources_child: int32 [128, 12], replicated, may hold values from 0 to 127
- kinds_child: int32 [128, 12], replicated, may hold values from 0 to 127
- table_child: float32 [2, 192, 384, 128], P(None, 'theta', 'phi'), may hold values from -4 to 4
- sources_parent: int32 [16, 12], replicated, may hold values from 0 to 15
- kinds_parent: int32 [16, 12], replicated, may hold values from 0 to 127
- table_parent: float32 [2, 352, 704, 128], P(None, 'theta', 'phi'), may hold values from -1.5 to 1.5
Outputs:
- child_in: float32 [8, 192, 384, 128], P(None, 'theta', 'phi')
The draws below stay inside these ranges and needn't reach their ends.
Inputs may be any that keep to these rules, and one draw needn't show every extreme that they name: Each value occurs once; child b belongs to parent child_slot[b] % 16 as octant child_slot[b] // 16.
All inputs are finite; a program needn't handle non-finite values.
Results may differ from the reference program's by a relative error of at most 0.00012.
Values sent between devices are 32-bit elements; how exact they have to be, the bound alone decides.
A program may use at most 128 MiB of HBM per device.

```python
import math
import jax
import jax.numpy as jnp
import numpy as np
from jax import lax

TH1 = 192
PH1 = 384
TH2 = 352
PH2 = 704
BAND1 = 180
NB1 = 128
NB2 = 16
LIST = 12
NTR = 128


def touch_ends(result, stream_key, least, high):
    index_at = [jax.random.randint(jax.random.fold_in(stream_key, axis), (), 0, length) for axis, length in enumerate(result.shape)]
    longest = result.shape.index(max(result.shape))
    beside = index_at[:longest] + [(index_at[longest] + 1) % result.shape[longest]] + index_at[longest + 1:]
    return result.at[tuple(index_at)].set(least).at[tuple(beside)].set(high)


def block_scale(key, dims, split, low, top_value):
    def one(axis_at, blocks):
        steps = jax.random.uniform(jax.random.fold_in(jax.random.fold_in(key, 6), axis_at), (blocks,), jnp.float32, low / len(split), top_value / len(split))
        return jnp.repeat(jnp.exp(steps), dims[axis_at] // blocks).reshape((-1,) + (1,) * (len(dims) - axis_at - 1))

    gain = one(*split[0])
    for cut in split[1:]:
        gain = gain * one(*cut)
    return gain


def scatter_about(rng, shape, spread, reach, pieces=(), kind=jnp.bfloat16):
    array = spread * jax.random.normal(rng, shape, jnp.float32)
    if pieces:
        array = array * block_scale(rng, shape, pieces, -0.22, 0.18)
    return jnp.clip(array, -reach, reach).astype(kind)


def setup_inputs(seed: int = 0) -> dict:
    key_list = jax.random.split(jax.random.key(seed), 9)
    return {
        "child_out": scatter_about(key_list[0], (8, TH1, PH1, NB1), 1.0, 6.0, ((1, 16), (2, 8)), jnp.float32),
        "child_slot": jax.random.permutation(key_list[1], NB1).astype(jnp.int32),
        "sources_child": touch_ends(jax.random.randint(key_list[2], (NB1, LIST), 0, NB1), jax.random.fold_in(key_list[2], 1), 0, NB1 - 1).astype(jnp.int32),
        "kinds_child": touch_ends(jax.random.randint(key_list[3], (NB1, LIST), 0, NTR), jax.random.fold_in(key_list[3], 1), 0, NTR - 1).astype(jnp.int32),
        "table_child": scatter_about(key_list[4], (2, TH1, PH1, NTR), 0.25, 4.0, ((1, 16), (2, 8)), jnp.float32),
        "sources_parent": touch_ends(jax.random.randint(key_list[5], (NB2, LIST), 0, NB2), jax.random.fold_in(key_list[5], 1), 0, NB2 - 1).astype(jnp.int32),
        "kinds_parent": touch_ends(jax.random.randint(key_list[6], (NB2, LIST), 0, NTR), jax.random.fold_in(key_list[6], 1), 0, NTR - 1).astype(jnp.int32),
        "table_parent": scatter_about(key_list[7], (2, TH2, PH2, NTR), 0.1, 1.5, ((1, 16), (2, 8)), jnp.float32),
    }


def stencil_entries(count_out, count_in, centered, out_rows):
    entries = []
    for row_out in out_rows:
        if centered:
            numerator = (2 * row_out + 1) * count_in - count_out
        else:
            numerator = 2 * row_out * count_in
        denominator = 2 * count_out
        base_index = numerator // denominator
        fraction = (numerator - base_index * denominator) / denominator
        for offset_a in range(-2, 4):
            weight = 1.0
            for offset_b in range(-2, 4):
                if offset_b != offset_a:
                    weight = weight * (fraction - offset_b) / (offset_a - offset_b)
            entries.append((row_out, base_index + offset_a, weight))
    return entries

def global_matrix(count_out, count_in, centered, periodic):
    matrix = np.zeros((count_out, count_in))
    for row_out, column, weight in stencil_entries(count_out, count_in, centered, range(count_out)):
        if periodic:
            matrix[row_out, column % count_in] += weight
        elif 0 <= column < count_in:
            matrix[row_out, column] += weight
    return jnp.asarray(matrix, jnp.float32)

def phase_table(count_polar, count_azimuth, polar_first, azimuth_first, rows_here, columns_here):
    polar = ((jnp.arange(rows_here, dtype=jnp.int32) + polar_first).astype(jnp.float32) + 0.5) * (math.pi / count_polar)
    azimuth = (jnp.arange(columns_here, dtype=jnp.int32) + azimuth_first).astype(jnp.float32) * (2.0 * math.pi / count_azimuth)
    octant = jnp.arange(8, dtype=jnp.int32)
    east_sign = (2 * (octant % 2) - 1).astype(jnp.float32)
    north_sign = (2 * (octant // 2 % 2) - 1).astype(jnp.float32)
    upper_sign = (2 * (octant // 4) - 1).astype(jnp.float32)
    sin_polar = jnp.sin(polar)[:, None, None]
    cos_polar = jnp.cos(polar)[:, None, None]
    cos_azimuth = jnp.cos(azimuth)[None, :, None]
    sin_azimuth = jnp.sin(azimuth)[None, :, None]
    phase_angle = BAND1 / (2.0 * math.sqrt(3.0)) * (sin_polar * cos_azimuth * east_sign + sin_polar * sin_azimuth * north_sign + cos_polar * upper_sign)
    return jnp.stack([jnp.cos(phase_angle), jnp.sin(phase_angle)])

def complex_times(pattern, factor):
    halves = pattern.reshape((2, 4) + pattern.shape[1:])
    cosine = factor[0][None]
    sine_part = factor[1][None]
    real_out = halves[0] * cosine - halves[1] * sine_part
    imag_out = halves[0] * sine_part + halves[1] * cosine
    return jnp.concatenate([real_out, imag_out], axis=0)

def aggregate(grouped, phase):
    halves = grouped.reshape((2, 4) + grouped.shape[1:])
    cosine = phase[0][None, :, :, :, None]
    sine_part = phase[1][None, :, :, :, None]
    real_out = lax.optimization_barrier(jnp.sum(halves[0] * cosine - halves[1] * sine_part, axis=3))
    imag_out = lax.optimization_barrier(jnp.sum(halves[0] * sine_part + halves[1] * cosine, axis=3))
    return jnp.concatenate([real_out, imag_out], axis=0)

def translate(pattern, sources, kinds, table):

    def accumulate(summed, columns):
        source_column, kind_column = columns
        gathered = jnp.take(pattern, source_column, axis=3)
        factor = jnp.take(table, kind_column, axis=3)
        return (summed + complex_times(gathered, factor), None)
    start = jnp.zeros(pattern.shape[:3] + (sources.shape[0],), jnp.float32)
    summed, unused = lax.scan(accumulate, start, (sources.T, kinds.T))
    return summed

def reference(child_out, child_slot, sources_child, kinds_child, table_child, sources_parent, kinds_parent, table_parent):
    exact_mode = lax.Precision.HIGHEST
    polar_up = global_matrix(TH2, TH1, True, False)
    azimuth_up = global_matrix(PH2, PH1, False, True)
    phase_up = phase_table(TH2, PH2, 0, 0, TH2, PH2)
    inverse = jnp.zeros((NB1,), jnp.int32).at[child_slot].set(jnp.arange(NB1, dtype=jnp.int32))
    children = inverse.reshape(8, NB2).T

    def one_parent(members):
        picked = jnp.take(child_out, members, axis=3)
        row_pass = jnp.einsum('pt,ctfo->cpfo', polar_up, picked, precision=exact_mode)
        interpolated = jnp.einsum('qf,cpfo->cpqo', azimuth_up, row_pass, precision=exact_mode)
        return aggregate(interpolated[..., None], phase_up)[..., 0]
    parents = lax.map(one_parent, children)
    parent_out = jnp.transpose(parents, (1, 2, 3, 0))
    parent_in = translate(parent_out, sources_parent, kinds_parent, table_parent)
    columns_back = jnp.einsum('qf,cpqb->cpfb', azimuth_up, parent_in, precision=exact_mode)
    lowered = jnp.einsum('pt,cpfb->ctfb', polar_up, columns_back, precision=exact_mode)
    expanded = jnp.take(lowered, child_slot % NB2, axis=3)
    phase_down = phase_table(TH1, PH1, 0, 0, TH1, PH1)
    box_phase = jnp.take(phase_down, child_slot // NB2, axis=3)
    factor = jnp.stack([box_phase[0], -box_phase[1]])
    child_local = translate(child_out, sources_child, kinds_child, table_child)
    return complex_times(expanded, factor) + child_local
```

```python
import functools
import math

import jax
import jax.numpy as jnp
import numpy as np
from jax import lax
from jax.experimental import pallas as pl
from jax.experimental.pallas import tpu as pltpu
from jax.sharding import PartitionSpec as P

TH1, PH1, TH2, PH2 = 192, 384, 352, 704
BAND1 = 180
LIST = 12
T1, F1, T2, F2 = 12, 48, 22, 88
QX = 96
NB = 128
ROWS = 32
WAVE = BAND1 / (2.0 * math.sqrt(3.0))
F32, BF16 = jnp.float32, jnp.bfloat16
MESH = pl.DeviceIdType.MESH
VM = pl.BlockSpec(memory_space=pltpu.VMEM)
SM = pl.BlockSpec(memory_space=pltpu.SMEM)


def stencil(count_out, count_in, centered, row_out):
    if centered:
        numerator = (2 * row_out + 1) * count_in - count_out
    else:
        numerator = 2 * row_out * count_in
    denominator = 2 * count_out
    base = numerator // denominator
    fraction = (numerator - base * denominator) / denominator
    weights = []
    for a in range(-2, 4):
        weight = 1.0
        for b in range(-2, 4):
            if b != a:
                weight = weight * (fraction - b) / (a - b)
        weights.append(weight)
    return base, weights


def as_halves(matrix):
    matrix = np.asarray(matrix, np.float32)
    high = matrix.astype(BF16)
    low = (matrix - high.astype(np.float32)).astype(BF16)
    return high, low


def parent_columns():
    return list(range(F2)) + [89, 90, 91, -5, -4, -3, -2, -1]


def child_columns():
    return list(range(F1)) + [48, 49, 50, None, None, -3, -2, -1]


def theta_weights():
    weight = np.zeros((ROWS * 6,), np.float32)
    for r in range(ROWS):
        base, weights = stencil(TH2, TH1, True, r - 5)
        for m in range(6):
            weight[r * 6 + m] = weights[m] if 0 <= base - 2 + m < T1 else 0.0
    return weight


def phi_up():
    matrix = np.zeros((QX, F1))
    for row, q in enumerate(parent_columns()):
        base, weights = stencil(PH2, PH1, False, q)
        for m in range(6):
            f = base - 2 + m
            if 0 <= f < F1:
                matrix[row, f] += weights[m]
    high, low = as_halves(matrix)
    return np.concatenate([high, high, low], axis=1)


def phi_down():
    matrix = np.zeros((56, 96))
    where = {f: row for row, f in enumerate(child_columns()) if f is not None}
    for q in range(F2):
        base, weights = stencil(PH2, PH1, False, q)
        for m in range(6):
            if weights[m] != 0.0:
                matrix[where[base - 2 + m], q] += weights[m]
    high, low = as_halves(matrix)
    return np.concatenate([high, high, low], axis=1)


def theta_down():
    slots = {}
    for t in range(T1):
        slots[t] = t
    for t in range(3):
        slots[12 + t] = 16 + t
        slots[t - 3] = 21 + t
    matrix = np.zeros((24, 24))
    for p in range(T2):
        base, weights = stencil(TH2, TH1, True, p)
        for m in range(6):
            matrix[p, slots[base - 2 + m]] += weights[m]
    big = np.kron(matrix, np.eye(16))
    high, low = as_halves(big)
    parts = []
    for tile in range(3):
        cut = slice(128 * tile, 128 * tile + 128)
        parts += [high[cut], high[cut], low[cut]]
    return np.concatenate(parts, axis=0)


def halves(x):
    high = x.astype(BF16)
    return high, (x - high.astype(F32)).astype(BF16)


def iota(shape, dim):
    return lax.broadcasted_iota(jnp.int32, shape, dim)


def flags(condition):
    return jnp.where(condition, 1.0, 0.0).astype(BF16)


def ring_phase(index, shift, period):
    value = index - shift
    value = jnp.where(value >= period, value - period, value)
    value = jnp.where(value >= period, value - period, value)
    value = jnp.where(value < 0, value + period, value)
    value = jnp.where(value < 0, value + period, value)
    angle = (value.astype(F32) + 0.5) * (2.0 * math.pi / period)
    phase = (WAVE / math.sqrt(2.0)) * jnp.sin(angle)
    return jnp.cos(phase), jnp.sin(phase)


def octant_shift(octant, eighth):
    east = octant % 2
    north = (octant // 2) % 2
    quarter = jnp.where(east == 1, eighth, 3 * eighth)
    return jnp.where(north == 1, quarter, -quarter)


def fill_phases(slot, tables, rows, first_plus, first_minus, polar_first, polar_rows, period):
    plus_c, plus_s, minus_c, minus_s, polar_c, polar_s = tables
    octant = jnp.broadcast_to(slot // 16, (rows, NB))
    shift = octant_shift(octant, period // 8)
    row = iota((rows, NB), 0)
    plus_c[...], plus_s[...] = ring_phase(row + first_plus, shift, period)
    minus_c[...], minus_s[...] = ring_phase(-(row + first_minus), -shift, period)
    upper = jnp.broadcast_to(slot // 64, (polar_rows, NB))
    sign = jnp.where(upper == 1, WAVE, -WAVE)
    polar = (iota((polar_rows, NB), 0) + polar_first).astype(F32) + 0.5
    phase = sign * jnp.cos(polar * (2.0 * math.pi / period))
    polar_c[...] = jnp.cos(phase)
    polar_s[...] = jnp.sin(phase)


def times(ar, ai, br, bi):
    return ar * br - ai * bi, ar * bi + ai * br


INDEX_ROWS = NB + 40


def index_kernel(slot_ref, sc_ref, kc_ref, sp_ref, kp_ref, o_ref, wide):
    o_ref[0:NB, :] = jnp.broadcast_to(slot_ref[...], (NB, NB)).T
    o_ref[NB : NB + 8, :] = jnp.broadcast_to(slot_ref[...], (8, NB))
    lane, row = iota((16, NB), 1), iota((16, NB), 0)
    wide[...] = jnp.zeros_like(wide)
    for n, ref in enumerate((sc_ref, kc_ref)):
        wide[:, 0:LIST] = ref[...]
        o_ref[NB + 8 + 16 * n : NB + 24 + 16 * n, :] = wide[...].T[0:16]
    wide[...] = jnp.zeros_like(wide)
    for n, ref in enumerate((sp_ref, kp_ref)):
        wide[0:16, 0:LIST] = ref[...]
        turned = wide[...].T[0:16].astype(F32)
        for step in (16, 32, 64):
            turned = turned + pltpu.roll(turned, step, 1)
        early = jnp.sum(jnp.where(row == lane // 16, turned, 0.0), axis=0, keepdims=True)
        late = jnp.sum(jnp.where(row == 8 + lax.rem(lane // 16, 4), turned, 0.0), axis=0, keepdims=True)
        o_ref[NB + 8 + 12 + 16 * n : NB + 9 + 12 + 16 * n, :] = early.astype(jnp.int32)
        o_ref[NB + 9 + 12 + 16 * n : NB + 10 + 12 + 16 * n, :] = late.astype(jnp.int32)


def up_setup(slot, slot_col, tables, group):
    theta, phi = lax.axis_index("theta"), lax.axis_index("phi")
    i0, k0 = theta * T2, phi * F2
    fill_phases(slot, tables, 136, i0 + k0 - 13, k0 - i0 - 34, i0 - 5, ROWS, PH2)
    parent = lax.rem(slot_col, 16)
    lane = iota((NB, NB), 1)
    for j in range(8):
        block = flags(lane == parent + 16 * j)
        group[j, 0:NB, :] = block
        group[j, NB : 2 * NB, :] = block


def up_rows(low, high, tile, slot_first, weight_ref, x_ref, up_ref, z_ref, rhs, lhs, group, tables):
    plus_c, plus_s, minus_c, minus_s, polar_c, polar_s = tables
    left = iota((8, NB), 0) >= 3

    def columns(table, start):
        main = table[pl.ds(start + 8, F2), :]
        edge = jnp.where(left, table[pl.ds(start, 8), :], table[pl.ds(start + 97, 8), :])
        return jnp.concatenate([main, edge], axis=0)

    def row(r, carry):
        base = (12 * (r - 5) - 5 + 110) // 22 - 5 - 2
        taps = [jnp.minimum(jnp.maximum(base + m, 0), T1 - 1) for m in range(6)]
        weights = [weight_ref[r * 6 + m] for m in range(6)]
        for c in range(8):
            y = weights[0] * x_ref[c, taps[0]]
            for m in range(1, 6):
                y = y + weights[m] * x_ref[c, taps[m]]
            hi, lo = halves(y)
            cut = slice(c * NB, c * NB + NB)
            rhs[0:F1, cut] = hi
            rhs[F1 : 2 * F1, cut] = lo
            rhs[2 * F1 : 3 * F1, cut] = hi
        v = jnp.dot(up_ref[...], rhs[...], preferred_element_type=F32)
        er, ei = times(
            columns(plus_c, r), columns(plus_s, r), columns(minus_c, 31 - r), columns(minus_s, 31 - r)
        )
        er, ei = times(er, ei, polar_c[pl.ds(r, 1), :], polar_s[pl.ds(r, 1), :])
        for c in range(4):
            vr, vi = v[:, c * NB : c * NB + NB], v[:, (c + 4) * NB : (c + 5) * NB]
            both = times(vr, vi, er, ei)
            for h in range(2):
                hi, lo = halves(both[h])
                cut = slice((c + 4 * h) * QX, (c + 4 * h + 1) * QX)
                lhs[cut, 0:NB] = hi
                lhs[cut, NB : 2 * NB] = lo
        summed = jnp.dot(lhs[...], group[r - low + slot_first], preferred_element_type=F32)
        z_ref[tile] = z_ref[tile] + summed.reshape(8, QX, NB)
        return carry

    lax.fori_loop(low, high, row, 0)


def neighbours():
    theta, phi = lax.axis_index("theta"), lax.axis_index("phi")
    last = lax.axis_size("theta") - 1
    ring = lax.axis_size("phi")
    right = lax.rem(phi + 1, ring)
    left = lax.rem(phi + ring - 1, ring)
    out = []
    for dt in (-1, 0, 1):
        for df, column in ((-1, left), (0, phi), (1, right)):
            if dt == 0 and df == 0:
                continue
            has = None if dt == 0 else (theta > 0 if dt < 0 else theta < last)
            out.append((dt, df, has, (theta + dt, column)))
    return out


def guarded(has, do):
    if has is None:
        do()
    else:
        pl.when(has)(do)


def greet(around):
    barrier = pltpu.get_barrier_semaphore()
    for dt, df, has, device in around:
        def signal(device=device):
            pl.semaphore_signal(barrier, inc=1, device_id=device, device_id_type=MESH)

        guarded(has, signal)


def met(around):
    barrier = pltpu.get_barrier_semaphore()
    inside = around[0][2] & around[-1][2]

    @pl.when(inside)
    def _():
        pl.semaphore_wait(barrier, 8)

    @pl.when(jnp.logical_not(inside))
    def _():
        pl.semaphore_wait(barrier, 5)


def exchange(around, wanted, source, landing, send_sem, recv_sem):
    for n, (dt, df, has, device) in enumerate(around):
        if wanted(dt):
            copy = pltpu.make_async_remote_copy(
                src_ref=source(dt, df),
                dst_ref=landing[(-dt, -df)],
                send_sem=send_sem.at[n],
                recv_sem=recv_sem.at[7 - n],
                device_id=device,
                device_id_type=MESH,
            )
            guarded(has, copy.start)


def finish(around, source, landing, send_sem, recv_sem):
    for n, (dt, df, has, device) in enumerate(around):
        copy = pltpu.make_async_remote_copy(
            src_ref=source(dt, df),
            dst_ref=landing[(dt, df)],
            send_sem=send_sem.at[n],
            recv_sem=recv_sem.at[n],
            device_id=device,
            device_id_type=MESH,
        )
        guarded(has, copy.wait)


STEP = 96


def child_setup(src_ref, kind_ref, hot_s, hot_k):
    row = lax.rem(iota((2 * NB, NB), 0), NB)
    for l in range(LIST):
        cut = slice(l * NB, l * NB + NB)
        hot_s[:, cut] = flags(row == src_ref[l : l + 1, :])
        hot_k[:, cut] = flags(row == kind_ref[l : l + 1, :])


def child_steps(low, high, x_ref, t_ref, o_ref, hot_s, hot_k, lx, lt):
    def step(g, carry):
        cut = pl.ds(2 * g, 2)
        for c in range(8):
            hi, lo = halves(x_ref[c, cut].reshape(STEP, NB))
            lx[c * STEP : (c + 1) * STEP, 0:NB] = hi
            lx[c * STEP : (c + 1) * STEP, NB : 2 * NB] = lo
        for c in range(2):
            hi, lo = halves(t_ref[c, cut].reshape(STEP, NB))
            lt[c * STEP : (c + 1) * STEP, 0:NB] = hi
            lt[c * STEP : (c + 1) * STEP, NB : 2 * NB] = lo
        total = [None] * 8
        for pair in range(LIST // 2):
            both = slice(pair * 2 * NB, (pair + 1) * 2 * NB)
            tt = jnp.dot(lt[...], hot_k[:, both], preferred_element_type=F32)
            xx = jnp.dot(lx[...], hot_s[:, both], preferred_element_type=F32)
            for h in range(2):
                one = slice(h * NB, h * NB + NB)
                a, b = tt[:STEP, one], tt[STEP:, one]
                for c in range(4):
                    u = xx[c * STEP : (c + 1) * STEP, one]
                    v = xx[(c + 4) * STEP : (c + 5) * STEP, one]
                    re, im = times(u, v, a, b)
                    total[c] = re if total[c] is None else total[c] + re
                    total[c + 4] = im if total[c + 4] is None else total[c + 4] + im
        for c in range(8):
            o_ref[c, cut] = total[c].reshape(2, F1, NB)
        return carry

    lax.fori_loop(low, high, step, 0)


def up_source(z_ref):
    def source(dt, df):
        if dt == 0:
            return z_ref.at[0:3, :, F2:QX, :]
        tile = 3 if dt < 0 else 4
        return z_ref.at[tile, :, 0:F2, :] if df == 0 else z_ref.at[tile, :, F2:QX, :]

    return source


def up_join(around, z_ref, landing):
    sub = iota((8, NB), 0)

    def from_left(tile, block):
        z_ref[tile, :, 0:8, :] += jnp.where((sub >= 1) & (sub <= 3), pltpu.roll(block, 1, 1), 0.0)

    def from_right(tile, block):
        z_ref[tile, :, F2 - 8 : F2, :] += jnp.where(sub >= 3, block, 0.0)

    for tile in range(3):
        from_left(tile, landing[(0, -1)][tile])
        from_right(tile, landing[(0, 1)][tile])

    @pl.when(around[0][2])
    def _():
        z_ref[0, :, 0:F2, :] += landing[(-1, 0)][...]
        from_left(0, landing[(-1, -1)][...])
        from_right(0, landing[(-1, 1)][...])

    @pl.when(around[-1][2])
    def _():
        z_ref[2, :, 0:F2, :] += landing[(1, 0)][...]
        from_left(2, landing[(1, -1)][...])
        from_right(2, landing[(1, 1)][...])


PAIRS = T2 // 2


def parent_setup(src_ref, kind_ref, hot_x, hot_a, hot_c, gather, inner, rd):
    lane = iota((NB, NB), 1)
    row = iota((NB, NB), 0)
    for half in range(2):
        cut = slice(half * NB, half * NB + NB)
        hot_a[cut, :] = flags(row == kind_ref[0:1, :])
        late = row == kind_ref[1:2, :]
        hot_c[0, cut, :] = flags(late & (lane < 64))
        hot_c[1, cut, :] = flags(late & (lane >= 64))
        for jj in range(4):
            hot_x[jj, cut, 0:NB] = flags(row == src_ref[0:1, :] + 32 * jj)
            hot_x[jj, cut, NB : 2 * NB] = flags(row == src_ref[0:1, :] + (32 * jj + 16))
            hot_x[jj, cut, 2 * NB : 3 * NB] = flags(row == src_ref[1:2, :] + (32 * jj + 16 * (lane // 64)))
    same = lax.rem(row, 16) == lax.rem(lane, 16)
    for jj in range(4):
        first = flags(same & (lane // 16 == 2 * jj))
        second = flags(same & (lane // 16 == 2 * jj + 1))
        third = flags(same & (lane // 16 == 2 * jj + row // 64))
        for half in range(2):
            gather[jj, half * NB : half * NB + NB, :] = first
            gather[jj, (2 + half) * NB : (3 + half) * NB, :] = second
            gather[jj, (4 + half) * NB : (5 + half) * NB, :] = third
    inner[...] = jnp.zeros_like(inner)
    rd[...] = jnp.zeros_like(rd)


def parent_rows(z_ref, t_ref, hot_x, hot_a, hot_c, gather, lx, lt, lp, inner):
    for tile in range(3):
        for c in range(8):
            hi, lo = halves(z_ref[tile, c, 0:F2, :])
            lx[tile, c * F2 : (c + 1) * F2, 0:NB] = hi
            lx[tile, c * F2 : (c + 1) * F2, NB : 2 * NB] = lo

    def pair(n, carry):
        tile, jj = n // 4, lax.rem(n, 4)
        for r in range(2):
            for c in range(2):
                hi, lo = halves(t_ref[c, 2 * n + r])
                lt[r, c * F2 : (c + 1) * F2, 0:NB] = hi
                lt[r, c * F2 : (c + 1) * F2, NB : 2 * NB] = lo
        tt = [
            jnp.dot(lt[0], hot_a[...], preferred_element_type=F32),
            jnp.dot(lt[1], hot_a[...], preferred_element_type=F32),
            jnp.dot(lt[0], hot_c[0], preferred_element_type=F32)
            + jnp.dot(lt[1], hot_c[1], preferred_element_type=F32),
        ]
        xx = jnp.dot(lx[tile], hot_x[jj], preferred_element_type=F32)
        for k in range(3):
            one = slice(k * NB, k * NB + NB)
            a, b = tt[k][:F2], tt[k][F2:]
            for c in range(4):
                u = xx[c * F2 : (c + 1) * F2, one]
                v = xx[(c + 4) * F2 : (c + 5) * F2, one]
                both = times(u, v, a, b)
                for h in range(2):
                    hi, lo = halves(both[h])
                    rows = slice((c + 4 * h) * F2, (c + 4 * h + 1) * F2)
                    lp[rows, 2 * k * NB : (2 * k + 1) * NB] = hi
                    lp[rows, (2 * k + 1) * NB : (2 * k + 2) * NB] = lo
        inner[tile] = inner[tile] + jnp.dot(lp[...], gather[jj], preferred_element_type=F32)
        return carry

    lax.fori_loop(0, PAIRS, pair, 0)


def parent_down(inner, theta_ref, phi_ref, w_ref, ld, rd):
    for tile in range(3):
        hi, lo = halves(inner[tile])
        ld[:, (3 * tile) * NB : (3 * tile + 1) * NB] = hi
        ld[:, (3 * tile + 1) * NB : (3 * tile + 2) * NB] = lo
        ld[:, (3 * tile + 2) * NB : (3 * tile + 3) * NB] = hi
    down = jnp.dot(ld[...], theta_ref[...], preferred_element_type=F32)
    for c in range(8):
        hi, lo = halves(down[c * F2 : (c + 1) * F2, :])
        cut = slice(c * 3 * NB, (c + 1) * 3 * NB)
        rd[0:F2, cut] = hi
        rd[96 : 96 + F2, cut] = lo
        rd[192 : 192 + F2, cut] = hi
    for c in range(8):
        cut = slice(c * 3 * NB, (c + 1) * 3 * NB)
        w_ref[c] = jnp.dot(phi_ref[...], rd[:, cut], preferred_element_type=F32)


def down_source(w_ref):
    def source(dt, df):
        rows = slice(0, F1) if df == 0 else slice(F1, 56)
        lanes = slice(0, 2 * NB) if dt == 0 else slice(2 * NB, 3 * NB)
        return w_ref.at[:, rows, lanes]

    return source


def down_join(around, w_ref, wo_ref, landing):
    wo_ref[...] = w_ref[:, 0:F1, 0 : 2 * NB]
    sub = iota((8, 2 * NB), 0)
    wo_ref[:, 0:8, :] += jnp.where(sub < 3, landing[(0, -1)][...], 0.0)
    wo_ref[:, F1 - 8 : F1, :] += jnp.where(sub >= 5, landing[(0, 1)][...], 0.0)
    lane = iota((F1, NB), 1)
    sub8, lane8 = iota((8, NB), 0), iota((8, NB), 1)

    @pl.when(around[0][2])
    def _():
        cut = slice(0, NB)
        wo_ref[:, :, cut] += jnp.where(lane < 48, landing[(-1, 0)][...], 0.0)
        wo_ref[:, 0:8, cut] += jnp.where((lane8 < 48) & (sub8 < 3), landing[(-1, -1)][...], 0.0)
        wo_ref[:, F1 - 8 : F1, cut] += jnp.where((lane8 < 48) & (sub8 >= 5), landing[(-1, 1)][...], 0.0)

    @pl.when(around[-1][2])
    def _():
        cut = slice(NB, 2 * NB)
        keep, keep8 = (lane >= 16) & (lane < 64), (lane8 >= 16) & (lane8 < 64)
        wo_ref[:, :, cut] += jnp.where(keep, pltpu.roll(landing[(1, 0)][...], 64, 2), 0.0)
        wo_ref[:, 0:8, cut] += jnp.where(keep8 & (sub8 < 3), pltpu.roll(landing[(1, -1)][...], 64, 2), 0.0)
        wo_ref[:, F1 - 8 : F1, cut] += jnp.where(keep8 & (sub8 >= 5), pltpu.roll(landing[(1, 1)][...], 64, 2), 0.0)


EARLY = 2


def main_kernel(weight_ref, index_ref, x_ref, tc_ref, tp_ref, up_ref, theta_ref, phi_ref, wo_ref, local_ref, *scratch):
    up_land, down_land, up_sems, down_sems = scratch[0:8], scratch[8:16], scratch[16:18], scratch[18:20]
    z_ref, rhs, lhs, group = scratch[20:24]
    tables = scratch[24:30]
    hot_s, hot_k, lx, lt = scratch[30:34]
    hot_x, hot_a, hot_c, gather, plx, plt, lp, inner, ld, rd, w_ref = scratch[34:45]
    keys = [(-1, 0), (1, 0), (0, -1), (0, 1), (-1, -1), (-1, 1), (1, -1), (1, 1)]
    up_landing, down_landing = dict(zip(keys, up_land)), dict(zip(keys, down_land))
    around = neighbours()
    greet(around)
    up_setup(index_ref[NB : NB + 1, :], index_ref[0:NB, :], tables, group)
    z_ref[...] = jnp.zeros_like(z_ref)
    shared = (weight_ref, x_ref, up_ref, z_ref, rhs, lhs, group, tables)
    up_rows(0, 5, 3, 1, *shared)
    up_rows(27, 32, 4, 0, *shared)
    child_setup(index_ref.at[NB + 8 : NB + 24], index_ref.at[NB + 24 : NB + 40], hot_s, hot_k)
    met(around)
    source = up_source(z_ref)
    exchange(around, lambda dt: dt != 0, source, up_landing, *up_sems)
    up_rows(5, 13, 0, 0, *shared)
    up_rows(13, 21, 1, 0, *shared)
    up_rows(21, 27, 2, 0, *shared)
    parent_setup(index_ref.at[NB + 20 : NB + 22], index_ref.at[NB + 36 : NB + 38], hot_x, hot_a, hot_c, gather, inner, rd)
    exchange(around, lambda dt: dt == 0, source, up_landing, *up_sems)
    children = (x_ref, tc_ref, local_ref, hot_s, hot_k, lx, lt)
    child_steps(0, EARLY, *children)
    finish(around, source, up_landing, *up_sems)
    up_join(around, z_ref, up_landing)
    parent_rows(z_ref, tp_ref, hot_x, hot_a, hot_c, gather, plx, plt, lp, inner)
    parent_down(inner, theta_ref, phi_ref, w_ref, ld, rd)
    source = down_source(w_ref)
    exchange(around, lambda dt: True, source, down_landing, *down_sems)
    child_steps(EARLY, T1 // 2, *children)
    finish(around, source, down_landing, *down_sems)
    down_join(around, w_ref, wo_ref, down_landing)


def final_kernel(slot_ref, w_ref, local_ref, o_ref, lw, spread, *tables):
    theta, phi = lax.axis_index("theta"), lax.axis_index("phi")
    t0, f0 = theta * T1, phi * F1
    fill_phases(slot_ref[...], tables, 64, t0 + f0, f0 - t0 - 11, t0, 16, PH1)
    plus_c, plus_s, minus_c, minus_s, polar_c, polar_s = tables
    row = iota((NB, NB), 0)
    parent = lax.rem(jnp.broadcast_to(slot_ref[...], (NB, NB)), 16)
    for j in range(8):
        block = flags(row == parent + 16 * j)
        spread[j, 0:NB, :] = block
        spread[j, NB : 2 * NB, :] = block
    for tile in range(2):
        for c in range(8):
            hi, lo = halves(w_ref[c, :, tile * NB : (tile + 1) * NB])
            lw[tile, c * F1 : (c + 1) * F1, 0:NB] = hi
            lw[tile, c * F1 : (c + 1) * F1, NB : 2 * NB] = lo

    def one_row(t, carry):
        wide = jnp.dot(lw[t // 8], spread[lax.rem(t, 8)], preferred_element_type=F32)
        er, ei = times(
            plus_c[pl.ds(t, F1), :],
            plus_s[pl.ds(t, F1), :],
            minus_c[pl.ds(11 - t, F1), :],
            minus_s[pl.ds(11 - t, F1), :],
        )
        er, ei = times(er, ei, polar_c[pl.ds(t, 1), :], polar_s[pl.ds(t, 1), :])
        for c in range(4):
            u, v = wide[c * F1 : (c + 1) * F1], wide[(c + 4) * F1 : (c + 5) * F1]
            re, im = times(u, v, er, -ei)
            o_ref[c, t] = re + local_ref[c, t]
            o_ref[c + 4, t] = im + local_ref[c + 4, t]
        return carry

    lax.fori_loop(0, T1, one_row, 0)


def phase_scratch(rows, polar_rows):
    return [pltpu.VMEM((rows, NB), F32)] * 4 + [pltpu.VMEM((polar_rows, NB), F32)] * 2


def shape(*dims):
    return jax.ShapeDtypeStruct(dims, F32)


def landing_scratch(column, row, corner):
    return [pltpu.VMEM(column, F32)] * 2 + [pltpu.VMEM(row, F32)] * 2 + [pltpu.VMEM(corner, F32)] * 4


def per_device(child_out, child_slot, sources_child, kinds_child, table_child, sources_parent, kinds_parent, table_parent):
    slot_row = child_slot.reshape(1, NB)
    params = dict(vmem_limit_bytes=60 * 1024 * 1024)
    index = pl.pallas_call(
        index_kernel,
        out_shape=jax.ShapeDtypeStruct((INDEX_ROWS, NB), jnp.int32),
        in_specs=[VM] * 5,
        out_specs=VM,
        scratch_shapes=[pltpu.VMEM((NB, NB), jnp.int32)],
        name="index",
    )(slot_row, sources_child, kinds_child, sources_parent, kinds_parent)

    wo, local = pl.pallas_call(
        main_kernel,
        out_shape=(shape(8, F1, 2 * NB), shape(8, T1, F1, NB)),
        in_specs=[SM] + [VM] * 7,
        out_specs=(VM, VM),
        scratch_shapes=landing_scratch((8, F2, NB), (3, 8, 8, NB), (8, 8, NB))
        + landing_scratch((8, F1, NB), (8, 8, 2 * NB), (8, 8, NB))
        + [pltpu.SemaphoreType.DMA((8,))] * 4
        + [
            pltpu.VMEM((5, 8, QX, NB), F32),
            pltpu.VMEM((3 * F1, 8 * NB), BF16),
            pltpu.VMEM((8 * QX, 2 * NB), BF16),
            pltpu.VMEM((8, 2 * NB, NB), BF16),
        ]
        + phase_scratch(136, ROWS)
        + [pltpu.VMEM((2 * NB, LIST * NB), BF16)] * 2
        + [pltpu.VMEM((8 * STEP, 2 * NB), BF16), pltpu.VMEM((2 * STEP, 2 * NB), BF16)]
        + [
            pltpu.VMEM((4, 2 * NB, 3 * NB), BF16),
            pltpu.VMEM((2 * NB, NB), BF16),
            pltpu.VMEM((2, 2 * NB, NB), BF16),
            pltpu.VMEM((4, 6 * NB, NB), BF16),
            pltpu.VMEM((3, 8 * F2, 2 * NB), BF16),
            pltpu.VMEM((2, 2 * F2, 2 * NB), BF16),
            pltpu.VMEM((8 * F2, 6 * NB), BF16),
            pltpu.VMEM((3, 8 * F2, NB), F32),
            pltpu.VMEM((8 * F2, 9 * NB), BF16),
            pltpu.VMEM((288, 8 * 3 * NB), BF16),
            pltpu.VMEM((8, 56, 3 * NB), F32),
        ],
        compiler_params=pltpu.CompilerParams(collective_id=0, has_side_effects=True, **params),
        name="main",
    )(
        jnp.asarray(theta_weights()),
        index,
        child_out,
        table_child,
        table_parent,
        jnp.asarray(phi_up()),
        jnp.asarray(theta_down()),
        jnp.asarray(phi_down()),
    )

    return pl.pallas_call(
        final_kernel,
        out_shape=shape(8, T1, F1, NB),
        in_specs=[VM] * 3,
        out_specs=VM,
        scratch_shapes=[pltpu.VMEM((2, 8 * F1, 2 * NB), BF16), pltpu.VMEM((8, 2 * NB, NB), BF16)]
        + phase_scratch(64, 16),
        compiler_params=pltpu.CompilerParams(**params),
        name="final",
    )(slot_row, wo, local)


def solution(mesh):
    block = P(None, "theta", "phi", None)
    return jax.shard_map(
        per_device,
        mesh=mesh,
        in_specs=(block, P(), P(), P(), block, P(), P(), block),
        out_specs=block,
        check_vma=False,
    )
```

```python
import functools
import math

import jax
import jax.numpy as jnp
import numpy as np
from jax import lax
from jax.experimental import pallas as pl
from jax.experimental.pallas import tpu as pltpu
from jax.sharding import PartitionSpec as P

TH1, PH1, TH2, PH2 = 192, 384, 352, 704
BAND1 = 180
LIST = 12
T1, F1, T2, F2 = 12, 48, 22, 88
QX = 96
NB = 128
ROWS = 34
WAVE = BAND1 / (2.0 * math.sqrt(3.0))
REVERSED = (0, 4, 2, 6, 1, 5, 3, 7)
F32, BF16 = jnp.float32, jnp.bfloat16
MESH = pl.DeviceIdType.MESH
VM = pl.BlockSpec(memory_space=pltpu.VMEM)
ANY = pl.BlockSpec(memory_space=pl.ANY)


def stencil(count_out, count_in, centered, row_out):
    if centered:
        numerator = (2 * row_out + 1) * count_in - count_out
    else:
        numerator = 2 * row_out * count_in
    denominator = 2 * count_out
    base = numerator // denominator
    fraction = (numerator - base * denominator) / denominator
    weights = []
    for a in range(-2, 4):
        weight = 1.0
        for b in range(-2, 4):
            if b != a:
                weight = weight * (fraction - b) / (a - b)
        weights.append(weight)
    return base, weights


def as_halves(matrix):
    matrix = np.asarray(matrix, np.float32)
    high = matrix.astype(BF16)
    low = (matrix - high.astype(np.float32)).astype(BF16)
    return high, low


def parent_columns():
    return list(range(F2)) + [89, 90, 91, -5, -4, -3, -2, -1]


def child_columns():
    return list(range(F1)) + [48, 49, 50, None, None, -3, -2, -1]


def theta_up(first, last, t_first, t_last):
    matrix = np.zeros((last - first, t_last - t_first))
    for p in range(first, last):
        base, weights = stencil(TH2, TH1, True, p)
        for m in range(6):
            t = base - 2 + m
            if 0 <= t < T1:
                matrix[p - first, t - t_first] += weights[m]
    high, low = as_halves(np.kron(matrix, np.eye(8)))
    return np.concatenate([high, high, low], axis=1)


BLOCKS = (
    (-6, 0, 0, 4, ((3, -6),)),
    (22, 28, 8, 12, ((4, 22),)),
    (0, 8, 0, 8, ((0, 0),)),
    (8, 22, 2, 12, ((1, 8), (2, 16))),
)


def phi_up():
    matrix = np.zeros((QX, F1))
    for row, q in enumerate(parent_columns()):
        base, weights = stencil(PH2, PH1, False, q)
        for m in range(6):
            f = base - 2 + m
            if 0 <= f < F1:
                matrix[row, f] += weights[m]
    high, low = as_halves(matrix)
    return np.concatenate([high, high, low], axis=1)


def phi_down():
    matrix = np.zeros((56, 96))
    where = {f: row for row, f in enumerate(child_columns()) if f is not None}
    for q in range(F2):
        base, weights = stencil(PH2, PH1, False, q)
        for m in range(6):
            if weights[m] != 0.0:
                matrix[where[base - 2 + m], q] += weights[m]
    high, low = as_halves(matrix)
    return np.concatenate([high, high, low], axis=1)


def theta_down():
    slots = {}
    for t in range(T1):
        slots[t] = t
    for t in range(3):
        slots[12 + t] = 16 + t
        slots[t - 3] = 21 + t
    matrix = np.zeros((24, 24))
    for p in range(T2):
        base, weights = stencil(TH2, TH1, True, p)
        for m in range(6):
            matrix[p, slots[base - 2 + m]] += weights[m]
    matrix = matrix[[8 * (g // 8) + REVERSED[g % 8] for g in range(24)]]
    big = np.kron(matrix, np.eye(16))
    high, low = as_halves(big)
    parts = []
    for tile in range(3):
        cut = slice(128 * tile, 128 * tile + 128)
        parts += [high[cut], high[cut], low[cut]]
    return np.concatenate(parts, axis=0)


def halves(x):
    high = x.astype(BF16)
    return high, (x - high.astype(F32)).astype(BF16)


def iota(shape, dim):
    return lax.broadcasted_iota(jnp.int32, shape, dim)


def flags(condition):
    return jnp.where(condition, 1.0, 0.0).astype(BF16)


def ring_phase(index, shift, period):
    value = index - shift
    value = jnp.where(value >= period, value - period, value)
    value = jnp.where(value >= period, value - period, value)
    value = jnp.where(value < 0, value + period, value)
    value = jnp.where(value < 0, value + period, value)
    angle = (value.astype(F32) + 0.5) * (2.0 * math.pi / period)
    phase = (WAVE / math.sqrt(2.0)) * jnp.sin(angle)
    return jnp.cos(phase), jnp.sin(phase)


def octant_shift(octant, eighth):
    east = octant % 2
    north = (octant // 2) % 2
    quarter = jnp.where(east == 1, eighth, 3 * eighth)
    return jnp.where(north == 1, quarter, -quarter)


def fill_phases(slot, tables, rows, first_plus, first_minus, polar_first, polar_rows, period):
    plus_c, plus_s, minus_c, minus_s, polar_c, polar_s = tables
    octant = jnp.broadcast_to(slot // 16, (rows, NB))
    shift = octant_shift(octant, period // 8)
    row = iota((rows, NB), 0)
    plus_c[...], plus_s[...] = ring_phase(row + first_plus, shift, period)
    minus_c[...], minus_s[...] = ring_phase(-(row + first_minus), -shift, period)
    upper = jnp.broadcast_to(slot // 64, (polar_rows, NB))
    sign = jnp.where(upper == 1, WAVE, -WAVE)
    polar = (iota((polar_rows, NB), 0) + polar_first).astype(F32) + 0.5
    phase = sign * jnp.cos(polar * (2.0 * math.pi / period))
    polar_c[...] = jnp.cos(phase)
    polar_s[...] = jnp.sin(phase)


def times(ar, ai, br, bi):
    return ar * br - ai * bi, ar * bi + ai * br


INDEX_ROWS = NB + 40


def index_kernel(slot_ref, sc_ref, kc_ref, sp_ref, kp_ref, o_ref, wide):
    o_ref[0:NB, :] = jnp.broadcast_to(slot_ref[...], (NB, NB)).T
    o_ref[NB : NB + 8, :] = jnp.broadcast_to(slot_ref[...], (8, NB))
    lane, row = iota((16, NB), 1), iota((16, NB), 0)
    for n, ref in enumerate((sc_ref, kc_ref)):
        o_ref[NB + 8 + 16 * n : NB + 8 + LIST + 16 * n, :] = ref[...]
    wide[...] = jnp.zeros_like(wide)
    for n, ref in enumerate((sp_ref, kp_ref)):
        wide[0:16, 0:LIST] = ref[...]
        turned = wide[...].T[0:16].astype(F32)
        for step in (16, 32, 64):
            turned = turned + pltpu.roll(turned, step, 1)
        early = jnp.sum(jnp.where(row == lane // 16, turned, 0.0), axis=0, keepdims=True)
        late = jnp.sum(jnp.where(row == 8 + lax.rem(lane // 16, 4), turned, 0.0), axis=0, keepdims=True)
        o_ref[NB + 8 + 12 + 16 * n : NB + 9 + 12 + 16 * n, :] = early.astype(jnp.int32)
        o_ref[NB + 9 + 12 + 16 * n : NB + 10 + 12 + 16 * n, :] = late.astype(jnp.int32)


def first_of_pair(m):
    lane = lax.rem(iota((1, NB), 1) + (128 - 32 * lax.rem(m, 2) - 16 * (m // 2)), 128)
    return lane < 64


def merge(keep, a, b, shift):
    return jnp.where(keep, a, b) + pltpu.roll(jnp.where(keep, b, a), shift, 1)


def merge_tile(pairs, count):
    lane = iota((1, NB), 1)
    first, second = lax.rem(lane, 64) < 32, lax.rem(lane + 112, 64) < 32
    even = lax.rem(lane, 32) < 16
    late = pairs[3] if count == 4 else jnp.zeros_like(pairs[2])
    return merge(even, merge(first, pairs[0], pairs[1], 96), merge(second, pairs[2], late, 96), 112)


def up_setup(slot_col, load_x, x_ref, up_ref, lhs, order, xh, xl, vh, vl, er_ref, ei_ref, tables):
    theta, phi = lax.axis_index("theta"), lax.axis_index("phi")
    i0, k0 = theta * T2, phi * F2
    fill_phases(iota((1, NB), 1), tables, 144, i0 + k0 - 14, k0 - i0 - 35, i0 - 6, 40, PH2)
    block = flags(iota((NB, NB), 1) == slot_col)
    order[...] = jnp.zeros_like(order)
    order[0:NB, 0:NB] = block
    order[NB : 2 * NB, NB : 2 * NB] = block

    load_x.wait()

    def turn(c, carry):
        hi, lo = halves(x_ref[c].reshape(T1 * F1, NB))
        lhs[:, 0:NB] = hi
        lhs[:, NB : 2 * NB] = lo
        out = jnp.dot(lhs[...], order[...], preferred_element_type=F32)
        xh[c] = out[:, 0:NB].astype(BF16).reshape(T1, F1, NB)
        xl[c] = out[:, NB : 2 * NB].astype(BF16).reshape(T1, F1, NB)
        return carry

    lax.fori_loop(0, 8, turn, 0)
    plus_c, plus_s, minus_c, minus_s, polar_c, polar_s = tables
    left = iota((8, NB), 0) >= 3

    def columns(table, start):
        main = table[pl.ds(start + 8, F2), :]
        edge = jnp.where(left, table[pl.ds(start, 8), :], table[pl.ds(start + 97, 8), :])
        return jnp.concatenate([main, edge], axis=0)

    def two_rows(n, carry):
        for c in range(4):
            outs = []
            for h in range(2):
                t = 2 * n + h
                high = jnp.concatenate([xh[c, t], xh[c + 4, t]], axis=1)
                low = jnp.concatenate([xl[c, t], xl[c + 4, t]], axis=1)
                rhs = jnp.concatenate([high, low, high], axis=0)
                outs.append(jnp.dot(up_ref[...], rhs, preferred_element_type=F32))
            at = pl.ds(pl.multiple_of(16 * n, 16), 16)
            for g in range(12):
                rows = slice(8 * g, 8 * g + 8)
                hi, lo = halves(jnp.concatenate([outs[0][rows], outs[1][rows]], axis=0))
                vh[g, c, at, :] = hi
                vl[g, c, at, :] = lo
        for extra in range(6):
            r = jnp.minimum(6 * n + extra, ROWS - 1)
            e = times(columns(plus_c, r), columns(plus_s, r), columns(minus_c, 33 - r), columns(minus_s, 33 - r))
            e = times(*e, polar_c[pl.ds(r, 1), :], polar_s[pl.ds(r, 1), :])
            er_ref[r], ei_ref[r] = e
        return carry

    lax.fori_loop(0, 6, two_rows, 0)


def up_blocks(numbers, theta_refs, z_ref, vh, vl, er_ref, ei_ref):
    keeps = [first_of_pair(m) for m in range(4)]

    def group(g, carry):
        rows = pl.ds(pl.multiple_of(8 * g, 8), 8)
        for number in numbers:
            first, last, t_first, t_last, tiles = BLOCKS[number]
            matrix = theta_refs[number]
            for c in range(4):
                part = slice(8 * t_first, 8 * t_last)
                high = vh[g, c, part, :]
                rhs = jnp.concatenate([high, vl[g, c, part, :], high], axis=0)
                v = jnp.dot(matrix[...], rhs, preferred_element_type=F32)
                for tile, start in tiles:
                    count = min(8, last - start) // 2
                    pairs = ([], [])
                    for m in range(count):
                        found = []
                        for p in (start + 2 * m, start + 2 * m + 1):
                            here = slice(8 * (p - first), 8 * (p - first) + 8)
                            e = er_ref[p + 6, rows, :], ei_ref[p + 6, rows, :]
                            found.append(times(v[here, 0:NB], v[here, NB : 2 * NB], *e))
                        for h in range(2):
                            pairs[h].append(merge(keeps[m], found[0][h], found[1][h], 64))
                    for h in range(2):
                        z_ref[tile, c + 4 * h, rows, :] = merge_tile(pairs[h], count)
        return carry

    lax.fori_loop(0, 12, group, 0)


def neighbours():
    theta, phi = lax.axis_index("theta"), lax.axis_index("phi")
    last = lax.axis_size("theta") - 1
    ring = lax.axis_size("phi")
    right = lax.rem(phi + 1, ring)
    left = lax.rem(phi + ring - 1, ring)
    out = []
    for dt in (-1, 0, 1):
        for df, column in ((-1, left), (0, phi), (1, right)):
            if dt == 0 and df == 0:
                continue
            has = None if dt == 0 else (theta > 0 if dt < 0 else theta < last)
            out.append((dt, df, has, (theta + dt, column)))
    return out


def guarded(has, do):
    if has is None:
        do()
    else:
        pl.when(has)(do)


def greet(around):
    barrier = pltpu.get_barrier_semaphore()
    for dt, df, has, device in around:
        def signal(device=device):
            pl.semaphore_signal(barrier, inc=1, device_id=device, device_id_type=MESH)

        guarded(has, signal)


def met(around):
    barrier = pltpu.get_barrier_semaphore()
    inside = around[0][2] & around[-1][2]

    @pl.when(inside)
    def _():
        pl.semaphore_wait(barrier, 8)

    @pl.when(jnp.logical_not(inside))
    def _():
        pl.semaphore_wait(barrier, 5)


def exchange(around, wanted, source, landing, send_sem, recv_sem):
    for n, (dt, df, has, device) in enumerate(around):
        if wanted(dt):
            copy = pltpu.make_async_remote_copy(
                src_ref=source(dt, df),
                dst_ref=landing[(-dt, -df)],
                send_sem=send_sem.at[n],
                recv_sem=recv_sem.at[7 - n],
                device_id=device,
                device_id_type=MESH,
            )
            guarded(has, copy.start)


def finish(around, source, landing, send_sem, recv_sem):
    for n, (dt, df, has, device) in enumerate(around):
        copy = pltpu.make_async_remote_copy(
            src_ref=source(dt, df),
            dst_ref=landing[(dt, df)],
            send_sem=send_sem.at[n],
            recv_sem=recv_sem.at[n],
            device_id=device,
            device_id_type=MESH,
        )
        guarded(has, copy.wait)


STEP = 96


def child_setup(src_ref, kind_ref, hot_s, hot_k):
    row = lax.rem(iota((2 * NB, NB), 0), NB)
    for l in range(LIST):
        cut = slice(l * NB, l * NB + NB)
        hot_s[:, cut] = flags(row == src_ref[l : l + 1, :])
        hot_k[:, cut] = flags(row == kind_ref[l : l + 1, :])


def child_steps(low, high, x_ref, t_ref, o_ref, hot_s, hot_k, lx, lt):
    def step(g, carry):
        cut = pl.ds(2 * g, 2)
        for c in range(8):
            hi, lo = halves(x_ref[c, cut].reshape(STEP, NB))
            lx[c * STEP : (c + 1) * STEP, 0:NB] = hi
            lx[c * STEP : (c + 1) * STEP, NB : 2 * NB] = lo
        for c in range(2):
            hi, lo = halves(t_ref[c, cut].reshape(STEP, NB))
            lt[c * STEP : (c + 1) * STEP, 0:NB] = hi
            lt[c * STEP : (c + 1) * STEP, NB : 2 * NB] = lo
        total = [None] * 8
        for pair in range(LIST // 2):
            both = slice(pair * 2 * NB, (pair + 1) * 2 * NB)
            tt = jnp.dot(lt[...], hot_k[:, both], preferred_element_type=F32)
            xx = jnp.dot(lx[...], hot_s[:, both], preferred_element_type=F32)
            for h in range(2):
                one = slice(h * NB, h * NB + NB)
                a, b = tt[:STEP, one], tt[STEP:, one]
                for c in range(4):
                    u = xx[c * STEP : (c + 1) * STEP, one]
                    v = xx[(c + 4) * STEP : (c + 5) * STEP, one]
                    re, im = times(u, v, a, b)
                    total[c] = re if total[c] is None else total[c] + re
                    total[c + 4] = im if total[c + 4] is None else total[c + 4] + im
        for c in range(8):
            o_ref[c, cut] = total[c].reshape(2, F1, NB)
        return carry

    lax.fori_loop(low, high, step, 0)


def up_source(z_ref):
    def source(dt, df):
        if dt == 0:
            return z_ref.at[0:3, :, F2:QX, :]
        tile = 3 if dt < 0 else 4
        return z_ref.at[tile, :, 0:F2, :] if df == 0 else z_ref.at[tile, :, F2:QX, :]

    return source


def up_join(around, z_ref, landing):
    sub = iota((8, NB), 0)

    def from_left(tile, block):
        z_ref[tile, :, 0:8, :] += jnp.where((sub >= 1) & (sub <= 3), pltpu.roll(block, 1, 1), 0.0)

    def from_right(tile, block):
        z_ref[tile, :, F2 - 8 : F2, :] += jnp.where(sub >= 3, block, 0.0)

    for tile in range(3):
        from_left(tile, landing[(0, -1)][tile])
        from_right(tile, landing[(0, 1)][tile])

    @pl.when(around[0][2])
    def _():
        z_ref[0, :, 0:F2, :] += landing[(-1, 0)][...]
        from_left(0, landing[(-1, -1)][...])
        from_right(0, landing[(-1, 1)][...])

    @pl.when(around[-1][2])
    def _():
        z_ref[2, :, 0:F2, :] += landing[(1, 0)][...]
        from_left(2, landing[(1, -1)][...])
        from_right(2, landing[(1, 1)][...])


PAIRS = T2 // 2


def parent_setup(src_ref, kind_ref, hot_x, hot_t, sums):
    row = iota((NB, NB), 0)
    for jj in range(4):
        keep = first_of_pair(jj)
        slot0, slot1 = REVERSED[2 * jj], REVERSED[2 * jj + 1]
        late_slot = jnp.where(keep, 16 * slot0, 16 * slot1)
        late = row == kind_ref[1:2, :]
        for half in range(2):
            cut = slice(half * NB, half * NB + NB)
            hot_x[jj, cut, 0:NB] = flags(row == src_ref[0:1, :] + 16 * slot0)
            hot_x[jj, cut, NB : 2 * NB] = flags(row == src_ref[0:1, :] + 16 * slot1)
            hot_x[jj, cut, 2 * NB : 3 * NB] = flags(row == src_ref[1:2, :] + late_slot)
            early = flags(row == kind_ref[0:1, :])
            hot_t[jj, 0, cut, 0:NB] = early
            hot_t[jj, 1, cut, 0:NB] = early
            hot_t[jj, 0, cut, NB : 2 * NB] = flags(late & keep)
            hot_t[jj, 1, cut, NB : 2 * NB] = flags(late & jnp.logical_not(keep))
    sums[11] = jnp.zeros_like(sums[11])


def parent_rows(z_ref, t_ref, hot_x, hot_t, lx, lt, sums):
    for tile in range(3):
        for c in range(8):
            hi, lo = halves(z_ref[tile, c, 0:F2, :])
            lx[tile, c * F2 : (c + 1) * F2, 0:NB] = hi
            lx[tile, c * F2 : (c + 1) * F2, NB : 2 * NB] = lo

    def pair(n, carry):
        tile, jj = n // 4, lax.rem(n, 4)
        keep = first_of_pair(jj)
        for r in range(2):
            for c in range(2):
                hi, lo = halves(t_ref[c, 2 * n + r])
                lt[r, c * F2 : (c + 1) * F2, 0:NB] = hi
                lt[r, c * F2 : (c + 1) * F2, NB : 2 * NB] = lo
        t0 = jnp.dot(lt[0], hot_t[jj, 0], preferred_element_type=F32)
        t1 = jnp.dot(lt[1], hot_t[jj, 1], preferred_element_type=F32)
        tt = [t0[:, 0:NB], t1[:, 0:NB], t0[:, NB : 2 * NB] + t1[:, NB : 2 * NB]]
        xx = jnp.dot(lx[tile], hot_x[jj], preferred_element_type=F32)
        for c in range(4):
            parts = []
            for k in range(3):
                one = slice(k * NB, k * NB + NB)
                u = xx[c * F2 : (c + 1) * F2, one]
                v = xx[(c + 4) * F2 : (c + 5) * F2, one]
                parts.append(times(u, v, tt[k][:F2], tt[k][F2:]))
            for h in range(2):
                value = merge(keep, parts[0][h], parts[1][h], 64) + parts[2][h]
                sums[n, (c + 4 * h) * F2 : (c + 4 * h + 1) * F2, :] = value
        return carry

    lax.fori_loop(0, PAIRS, pair, 0)


def parent_down(sums, theta_ref, phi_ref, w_ref, ld, rd):
    for tile in range(3):
        hi, lo = halves(merge_tile([sums[4 * tile + m] for m in range(4)], 4))
        ld[:, (3 * tile) * NB : (3 * tile + 1) * NB] = hi
        ld[:, (3 * tile + 1) * NB : (3 * tile + 2) * NB] = lo
        ld[:, (3 * tile + 2) * NB : (3 * tile + 3) * NB] = hi
    down = jnp.dot(ld[...], theta_ref[...], preferred_element_type=F32)
    for c in range(8):
        hi, lo = halves(down[c * F2 : (c + 1) * F2, :])
        cut = slice(c * 3 * NB, (c + 1) * 3 * NB)
        rd[0:F2, cut] = hi
        rd[96 : 96 + F2, cut] = lo
        rd[192 : 192 + F2, cut] = hi
    for c in range(8):
        cut = slice(c * 3 * NB, (c + 1) * 3 * NB)
        w_ref[c] = jnp.dot(phi_ref[...], rd[:, cut], preferred_element_type=F32)


def down_pack(w_ref, send_up, send_down):
    low = iota((F1 // 2, NB), 1) < 64
    for c in range(8):
        near = w_ref[c, 0 : F1 // 2, 2 * NB : 3 * NB]
        far = pltpu.roll(w_ref[c, F1 // 2 : F1, 2 * NB : 3 * NB], 64, 1)
        send_up[c] = jnp.where(low, near, far)
        send_down[c] = jnp.where(low, far, near)


def down_source(w_ref, send_up, send_down):
    def source(dt, df):
        if df == 0:
            return send_up if dt > 0 else send_down
        if dt == 0:
            return w_ref.at[:, F1:56, 0 : 2 * NB]
        return w_ref.at[:, F1:56, 2 * NB : 3 * NB]

    return source


def down_join(around, w_ref, wo_ref, landing):
    wo_ref[...] = w_ref[:, 0:F1, 0 : 2 * NB]
    sub = iota((8, 2 * NB), 0)
    wo_ref[:, 0:8, :] += jnp.where(sub < 3, landing[(0, -1)][...], 0.0)
    wo_ref[:, F1 - 8 : F1, :] += jnp.where(sub >= 5, landing[(0, 1)][...], 0.0)
    half = F1 // 2
    lane = iota((half, NB), 1)
    sub8, lane8 = iota((8, NB), 0), iota((8, NB), 1)

    @pl.when(around[0][2])
    def _():
        cut = slice(0, NB)
        for c in range(8):
            got = landing[(-1, 0)][c]
            wo_ref[c, 0:half, cut] += jnp.where(lane < 48, got, 0.0)
            wo_ref[c, half:F1, cut] += jnp.where(lane < 48, pltpu.roll(got, 64, 1), 0.0)
        wo_ref[:, 0:8, cut] += jnp.where((lane8 < 48) & (sub8 < 3), landing[(-1, -1)][...], 0.0)
        wo_ref[:, F1 - 8 : F1, cut] += jnp.where((lane8 < 48) & (sub8 >= 5), landing[(-1, 1)][...], 0.0)

    @pl.when(around[-1][2])
    def _():
        cut = slice(NB, 2 * NB)
        keep, keep8 = (lane >= 16) & (lane < 64), (lane8 >= 16) & (lane8 < 64)
        for c in range(8):
            got = landing[(1, 0)][c]
            wo_ref[c, 0:half, cut] += jnp.where(keep, pltpu.roll(got, 64, 1), 0.0)
            wo_ref[c, half:F1, cut] += jnp.where(keep, got, 0.0)
        wo_ref[:, 0:8, cut] += jnp.where(keep8 & (sub8 < 3), pltpu.roll(landing[(1, -1)][...], 64, 2), 0.0)
        wo_ref[:, F1 - 8 : F1, cut] += jnp.where(keep8 & (sub8 >= 5), pltpu.roll(landing[(1, 1)][...], 64, 2), 0.0)


EARLY = 2


def main_kernel(
    index_ref, x_far, tc_far, tp_far, theta_far, up_ref, ta_ref, tb_ref, tc2_ref, td_ref, phi_ref, wo_ref, local_far, *scratch
):
    up_land, down_land, up_sems, down_sems = scratch[0:8], scratch[8:16], scratch[16:18], scratch[18:20]
    z_ref, lhs, order, xh, xl, vh, vl, er_ref, ei_ref = scratch[20:29]
    tables = scratch[29:35]
    hot_s, hot_k, lx, lt = scratch[35:39]
    hot_x, hot_t, plx, plt, sums, ld, rd, w_ref = scratch[39:47]
    x_ref, tc_ref, tp_ref, theta_ref, local_ref, send_up, send_down, load_sem, store_sem = scratch[47:56]
    loads = [
        pltpu.make_async_copy(far, near, load_sem.at[n])
        for n, (far, near) in enumerate(
            ((x_far, x_ref), (tc_far, tc_ref), (tp_far, tp_ref), (theta_far, theta_ref))
        )
    ]
    stores = [
        pltpu.make_async_copy(local_ref.at[:, rows], local_far.at[:, rows], store_sem.at[n])
        for n, rows in enumerate((slice(0, 2 * EARLY), slice(2 * EARLY, T1)))
    ]
    for load in loads:
        load.start()
    keys = [(-1, 0), (1, 0), (0, -1), (0, 1), (-1, -1), (-1, 1), (1, -1), (1, 1)]
    up_landing, down_landing = dict(zip(keys, up_land)), dict(zip(keys, down_land))
    around = neighbours()
    greet(around)
    up_setup(index_ref[0:NB, :], loads[0], x_ref, up_ref, lhs, order, xh, xl, vh, vl, er_ref, ei_ref, tables)
    shared = ((ta_ref, tb_ref, tc2_ref, td_ref), z_ref, vh, vl, er_ref, ei_ref)
    up_blocks((0, 1), *shared)
    child_setup(index_ref.at[NB + 8 : NB + 24], index_ref.at[NB + 24 : NB + 40], hot_s, hot_k)
    met(around)
    source = up_source(z_ref)
    exchange(around, lambda dt: dt != 0, source, up_landing, *up_sems)
    up_blocks((2, 3), *shared)
    rd[...] = jnp.zeros_like(rd)
    parent_setup(index_ref.at[NB + 20 : NB + 22], index_ref.at[NB + 36 : NB + 38], hot_x, hot_t, sums)
    exchange(around, lambda dt: dt == 0, source, up_landing, *up_sems)
    children = (x_ref, tc_ref, local_ref, hot_s, hot_k, lx, lt)
    loads[1].wait()
    child_steps(0, EARLY, *children)
    stores[0].start()
    finish(around, source, up_landing, *up_sems)
    up_join(around, z_ref, up_landing)
    loads[2].wait()
    loads[3].wait()
    parent_rows(z_ref, tp_ref, hot_x, hot_t, plx, plt, sums)
    parent_down(sums, theta_ref, phi_ref, w_ref, ld, rd)
    down_pack(w_ref, send_up, send_down)
    source = down_source(w_ref, send_up, send_down)
    exchange(around, lambda dt: True, source, down_landing, *down_sems)
    child_steps(EARLY, T1 // 2, *children)
    stores[1].start()
    finish(around, source, down_landing, *down_sems)
    down_join(around, w_ref, wo_ref, down_landing)
    for store in stores:
        store.wait()


FINAL = 2


def final_kernel(slot_ref, w_ref, local_ref, o_ref, lw, spread, *tables):
    plus_c, plus_s, minus_c, minus_s, polar_c, polar_s = tables

    @pl.when(pl.program_id(0) == 0)
    def _():
        theta, phi = lax.axis_index("theta"), lax.axis_index("phi")
        t0, f0 = theta * T1, phi * F1
        fill_phases(slot_ref[...], tables, 64, t0 + f0, f0 - t0 - 11, t0, 16, PH1)
        row = iota((NB, NB), 0)
        parent = lax.rem(jnp.broadcast_to(slot_ref[...], (NB, NB)), 16)
        for j in range(8):
            block = flags(row == parent + 16 * j)
            spread[j, 0:NB, :] = block
            spread[j, NB : 2 * NB, :] = block
        for tile in range(2):
            for c in range(8):
                hi, lo = halves(w_ref[c, :, tile * NB : (tile + 1) * NB])
                lw[tile, c * F1 : (c + 1) * F1, 0:NB] = hi
                lw[tile, c * F1 : (c + 1) * F1, NB : 2 * NB] = lo

    for n in range(FINAL):
        t = pl.program_id(0) * FINAL + n
        wide = jnp.dot(lw[t // 8], spread[lax.rem(t, 8)], preferred_element_type=F32)
        er, ei = times(
            plus_c[pl.ds(t, F1), :],
            plus_s[pl.ds(t, F1), :],
            minus_c[pl.ds(11 - t, F1), :],
            minus_s[pl.ds(11 - t, F1), :],
        )
        er, ei = times(er, ei, polar_c[pl.ds(t, 1), :], polar_s[pl.ds(t, 1), :])
        for c in range(4):
            u, v = wide[c * F1 : (c + 1) * F1], wide[(c + 4) * F1 : (c + 5) * F1]
            re, im = times(u, v, er, -ei)
            o_ref[c, n] = re + local_ref[c, n]
            o_ref[c + 4, n] = im + local_ref[c + 4, n]


def phase_scratch(rows, polar_rows):
    return [pltpu.VMEM((rows, NB), F32)] * 4 + [pltpu.VMEM((polar_rows, NB), F32)] * 2


def shape(*dims):
    return jax.ShapeDtypeStruct(dims, F32)


def landing_scratch(column, row, corner):
    return [pltpu.VMEM(column, F32)] * 2 + [pltpu.VMEM(row, F32)] * 2 + [pltpu.VMEM(corner, F32)] * 4


def per_device(child_out, child_slot, sources_child, kinds_child, table_child, sources_parent, kinds_parent, table_parent):
    slot_row = child_slot.reshape(1, NB)
    params = dict(vmem_limit_bytes=60 * 1024 * 1024)
    index = pl.pallas_call(
        index_kernel,
        out_shape=jax.ShapeDtypeStruct((INDEX_ROWS, NB), jnp.int32),
        in_specs=[VM] * 5,
        out_specs=VM,
        scratch_shapes=[pltpu.VMEM((NB, NB), jnp.int32)],
        name="index",
    )(slot_row, sources_child.T, kinds_child.T, sources_parent, kinds_parent)

    wo, local = pl.pallas_call(
        main_kernel,
        out_shape=(shape(8, F1, 2 * NB), shape(8, T1, F1, NB)),
        in_specs=[VM] + [ANY] * 4 + [VM] * 6,
        out_specs=(VM, ANY),
        scratch_shapes=landing_scratch((8, F2, NB), (3, 8, 8, NB), (8, 8, NB))
        + landing_scratch((8, F1 // 2, NB), (8, 8, 2 * NB), (8, 8, NB))
        + [pltpu.SemaphoreType.DMA((8,))] * 4
        + [
            pltpu.VMEM((5, 8, QX, NB), F32),
            pltpu.VMEM((T1 * F1, 2 * NB), BF16),
            pltpu.VMEM((2 * NB, 2 * NB), BF16),
            pltpu.VMEM((8, T1, F1, NB), BF16),
            pltpu.VMEM((8, T1, F1, NB), BF16),
            pltpu.VMEM((12, 4, 8 * T1, 2 * NB), BF16),
            pltpu.VMEM((12, 4, 8 * T1, 2 * NB), BF16),
            pltpu.VMEM((ROWS, QX, NB), F32),
            pltpu.VMEM((ROWS, QX, NB), F32),
        ]
        + phase_scratch(144, 40)
        + [pltpu.VMEM((2 * NB, LIST * NB), BF16)] * 2
        + [pltpu.VMEM((8 * STEP, 2 * NB), BF16), pltpu.VMEM((2 * STEP, 2 * NB), BF16)]
        + [
            pltpu.VMEM((4, 2 * NB, 3 * NB), BF16),
            pltpu.VMEM((4, 2, 2 * NB, 2 * NB), BF16),
            pltpu.VMEM((3, 8 * F2, 2 * NB), BF16),
            pltpu.VMEM((2, 2 * F2, 2 * NB), BF16),
            pltpu.VMEM((12, 8 * F2, NB), F32),
            pltpu.VMEM((8 * F2, 9 * NB), BF16),
            pltpu.VMEM((288, 8 * 3 * NB), BF16),
            pltpu.VMEM((8, 56, 3 * NB), F32),
            pltpu.VMEM((8, T1, F1, NB), F32),
            pltpu.VMEM((2, T1, F1, NB), F32),
            pltpu.VMEM((2, T2, F2, NB), F32),
            pltpu.VMEM((9 * NB, 3 * NB), BF16),
            pltpu.VMEM((8, T1, F1, NB), F32),
            pltpu.VMEM((8, F1 // 2, NB), F32),
            pltpu.VMEM((8, F1 // 2, NB), F32),
            pltpu.SemaphoreType.DMA((4,)),
            pltpu.SemaphoreType.DMA((2,)),
        ],
        compiler_params=pltpu.CompilerParams(collective_id=0, has_side_effects=True, **params),
        name="main",
    )(
        index,
        child_out,
        table_child,
        table_parent,
        jnp.asarray(theta_down()),
        jnp.asarray(phi_up()),
        *[jnp.asarray(theta_up(*block[:4])) for block in BLOCKS],
        jnp.asarray(phi_down()),
    )

    return pl.pallas_call(
        final_kernel,
        grid=(T1 // FINAL,),
        out_shape=shape(8, T1, F1, NB),
        in_specs=[
            pl.BlockSpec((1, NB), lambda n: (0, 0)),
            pl.BlockSpec((8, F1, 2 * NB), lambda n: (0, 0, 0)),
            pl.BlockSpec((8, FINAL, F1, NB), lambda n: (0, n, 0, 0)),
        ],
        out_specs=pl.BlockSpec((8, FINAL, F1, NB), lambda n: (0, n, 0, 0)),
        scratch_shapes=[pltpu.VMEM((2, 8 * F1, 2 * NB), BF16), pltpu.VMEM((8, 2 * NB, NB), BF16)]
        + phase_scratch(64, 16),
        compiler_params=pltpu.CompilerParams(**params),
        name="final",
    )(slot_row, wo, local)


def solution(mesh):
    block = P(None, "theta", "phi", None)
    return jax.shard_map(
        per_device,
        mesh=mesh,
        in_specs=(block, P(), P(), P(), block, P(), P(), block),
        out_specs=block,
        check_vma=False,
    )
```

```python
import functools
import math

import jax
import jax.numpy as jnp
import numpy as np
from jax import lax
from jax.experimental import pallas as pl
from jax.experimental.pallas import tpu as pltpu
from jax.sharding import PartitionSpec as P

TH1, PH1, TH2, PH2 = 192, 384, 352, 704
BAND1 = 180
LIST = 12
T1, F1, T2, F2 = 12, 48, 22, 88
QX = 96
NB = 128
ROWS = 34
WAVE = BAND1 / (2.0 * math.sqrt(3.0))
REVERSED = (0, 4, 2, 6, 1, 5, 3, 7)
F32, BF16 = jnp.float32, jnp.bfloat16
MESH = pl.DeviceIdType.MESH
VM = pl.BlockSpec(memory_space=pltpu.VMEM)
ANY = pl.BlockSpec(memory_space=pl.ANY)


def stencil(count_out, count_in, centered, row_out):
    if centered:
        numerator = (2 * row_out + 1) * count_in - count_out
    else:
        numerator = 2 * row_out * count_in
    denominator = 2 * count_out
    base = numerator // denominator
    fraction = (numerator - base * denominator) / denominator
    weights = []
    for a in range(-2, 4):
        weight = 1.0
        for b in range(-2, 4):
            if b != a:
                weight = weight * (fraction - b) / (a - b)
        weights.append(weight)
    return base, weights


def as_halves(matrix):
    matrix = np.asarray(matrix, np.float32)
    high = matrix.astype(BF16)
    low = (matrix - high.astype(np.float32)).astype(BF16)
    return high, low


def parent_columns():
    return list(range(F2)) + [89, 90, 91, -5, -4, -3, -2, -1]


def child_columns():
    return list(range(F1)) + [48, 49, 50, None, None, -3, -2, -1]


def theta_up(first, last, t_first, t_last):
    matrix = np.zeros((last - first, t_last - t_first))
    for p in range(first, last):
        base, weights = stencil(TH2, TH1, True, p)
        for m in range(6):
            t = base - 2 + m
            if 0 <= t < T1:
                matrix[p - first, t - t_first] += weights[m]
    high, low = as_halves(np.kron(matrix, np.eye(8)))
    return np.concatenate([high, high, low], axis=1)


BLOCKS = (
    (-6, 0, 0, 4, ((3, -6),)),
    (22, 28, 8, 12, ((4, 22),)),
    (0, 8, 0, 8, ((0, 0),)),
    (8, 22, 2, 12, ((1, 8), (2, 16))),
)


def phi_up():
    matrix = np.zeros((QX, F1))
    for row, q in enumerate(parent_columns()):
        base, weights = stencil(PH2, PH1, False, q)
        for m in range(6):
            f = base - 2 + m
            if 0 <= f < F1:
                matrix[row, f] += weights[m]
    high, low = as_halves(matrix)
    return np.concatenate([high, high, low], axis=1)


def phi_down():
    matrix = np.zeros((56, 96))
    where = {f: row for row, f in enumerate(child_columns()) if f is not None}
    for q in range(F2):
        base, weights = stencil(PH2, PH1, False, q)
        for m in range(6):
            if weights[m] != 0.0:
                matrix[where[base - 2 + m], q] += weights[m]
    high, low = as_halves(matrix)
    return np.concatenate([high, high, low], axis=1)


def theta_down():
    slots = {}
    for t in range(T1):
        slots[t] = t
    for t in range(3):
        slots[12 + t] = 16 + t
        slots[t - 3] = 21 + t
    matrix = np.zeros((24, 24))
    for p in range(T2):
        base, weights = stencil(TH2, TH1, True, p)
        for m in range(6):
            matrix[p, slots[base - 2 + m]] += weights[m]
    matrix = matrix[[8 * (g // 8) + REVERSED[g % 8] for g in range(24)]]
    big = np.kron(matrix, np.eye(16))
    high, low = as_halves(big)
    parts = []
    for tile in range(3):
        cut = slice(128 * tile, 128 * tile + 128)
        parts += [high[cut], high[cut], low[cut]]
    return np.concatenate(parts, axis=0)


def halves(x):
    high = x.astype(BF16)
    return high, (x - high.astype(F32)).astype(BF16)


def iota(shape, dim):
    return lax.broadcasted_iota(jnp.int32, shape, dim)


def flags(condition):
    return jnp.where(condition, 1.0, 0.0).astype(BF16)


def ring_phase(index, shift, period):
    value = index - shift
    value = jnp.where(value >= period, value - period, value)
    value = jnp.where(value >= period, value - period, value)
    value = jnp.where(value < 0, value + period, value)
    value = jnp.where(value < 0, value + period, value)
    angle = (value.astype(F32) + 0.5) * (2.0 * math.pi / period)
    phase = (WAVE / math.sqrt(2.0)) * jnp.sin(angle)
    return jnp.cos(phase), jnp.sin(phase)


def octant_shift(octant, eighth):
    east = octant % 2
    north = (octant // 2) % 2
    quarter = jnp.where(east == 1, eighth, 3 * eighth)
    return jnp.where(north == 1, quarter, -quarter)


UP_ROWS, DOWN_ROWS = (144, 40), (64, 16)


def table_rows(rows):
    starts = [0, rows[0], 2 * rows[0], 3 * rows[0], 4 * rows[0], 4 * rows[0] + rows[1]]
    return starts, 4 * rows[0] + 2 * rows[1]


def views(ref, rows):
    starts, end = table_rows(rows)
    return [ref.at[low:high] for low, high in zip(starts, starts[1:] + [end])]


def fill_phases(octant, o_ref, rows, first_plus, first_minus, polar_first, period):
    starts, end = table_rows(rows)
    lane = iota((8, NB), 1)
    shift = octant_shift(lane // 16, period // 8)
    sign = jnp.where(lane // 64 == 1, WAVE, -WAVE)
    for n in range(0, max(rows), 128):
        row = n + 8 * lax.rem(lane, 16) + iota((8, NB), 0)
        polar = (row + polar_first).astype(F32) + 0.5
        phase = sign * jnp.cos(polar * (2.0 * math.pi / period))
        packed = (
            *ring_phase(row + first_plus, shift, period),
            *ring_phase(-(row + first_minus), -shift, period),
            jnp.cos(phase),
            jnp.sin(phase),
        )
        for k in range(6):
            for j in range(min(16, (rows[k // 4] - n) // 8)):
                spread = jnp.take_along_axis(packed[k], octant * 16 + j, axis=1)
                o_ref[starts[k] + n + 8 * j : starts[k] + n + 8 * j + 8, :] = spread


def times(ar, ai, br, bi):
    return ar * br - ai * bi, ar * bi + ai * br


INDEX_ROWS = NB + 40


def index_kernel(slot_ref, sc_ref, kc_ref, sp_ref, kp_ref, o_ref, up_ref, down_ref, wide):
    theta, phi = lax.axis_index("theta"), lax.axis_index("phi")
    i0, k0 = theta * T2, phi * F2
    fill_phases(iota((8, NB), 1) // 16, up_ref, UP_ROWS, i0 + k0 - 14, k0 - i0 - 35, i0 - 6, PH2)
    t0, f0 = theta * T1, phi * F1
    octant = jnp.broadcast_to(slot_ref[...] // 16, (8, NB))
    fill_phases(octant, down_ref, DOWN_ROWS, t0 + f0, f0 - t0 - 11, t0, PH1)
    o_ref[0:NB, :] = jnp.broadcast_to(slot_ref[...], (NB, NB)).T
    o_ref[NB : NB + 8, :] = jnp.broadcast_to(slot_ref[...], (8, NB))
    lane, row = iota((16, NB), 1), iota((16, NB), 0)
    for n, ref in enumerate((sc_ref, kc_ref)):
        o_ref[NB + 8 + 16 * n : NB + 8 + LIST + 16 * n, :] = ref[...]
    wide[...] = jnp.zeros_like(wide)
    for n, ref in enumerate((sp_ref, kp_ref)):
        wide[0:16, 0:LIST] = ref[...]
        turned = wide[...].T[0:16].astype(F32)
        for step in (16, 32, 64):
            turned = turned + pltpu.roll(turned, step, 1)
        early = jnp.sum(jnp.where(row == lane // 16, turned, 0.0), axis=0, keepdims=True)
        late = jnp.sum(jnp.where(row == 8 + lax.rem(lane // 16, 4), turned, 0.0), axis=0, keepdims=True)
        o_ref[NB + 8 + 12 + 16 * n : NB + 9 + 12 + 16 * n, :] = early.astype(jnp.int32)
        o_ref[NB + 9 + 12 + 16 * n : NB + 10 + 12 + 16 * n, :] = late.astype(jnp.int32)


def first_of_pair(m):
    lane = lax.rem(iota((1, NB), 1) + (128 - 32 * lax.rem(m, 2) - 16 * (m // 2)), 128)
    return lane < 64


def merge(keep, a, b, shift):
    return jnp.where(keep, a, b) + pltpu.roll(jnp.where(keep, b, a), shift, 1)


def merge_tile(pairs, count):
    lane = iota((1, NB), 1)
    first, second = lax.rem(lane, 64) < 32, lax.rem(lane + 112, 64) < 32
    even = lax.rem(lane, 32) < 16
    late = pairs[3] if count == 4 else jnp.zeros_like(pairs[2])
    return merge(even, merge(first, pairs[0], pairs[1], 96), merge(second, pairs[2], late, 96), 112)


def up_turn(slot_col, load_x, x_ref, lhs, order, xh, xl):
    block = flags(iota((NB, NB), 1) == slot_col)
    order[...] = jnp.zeros_like(order)
    order[0:NB, 0:NB] = block
    order[NB : 2 * NB, NB : 2 * NB] = block

    load_x.wait()

    def turn(c, carry):
        hi, lo = halves(x_ref[c].reshape(T1 * F1, NB))
        lhs[:, 0:NB] = hi
        lhs[:, NB : 2 * NB] = lo
        out = jnp.dot(lhs[...], order[...], preferred_element_type=F32)
        xh[c] = out[:, 0:NB].astype(BF16).reshape(T1, F1, NB)
        xl[c] = out[:, NB : 2 * NB].astype(BF16).reshape(T1, F1, NB)
        return carry

    lax.fori_loop(0, 8, turn, 0)


def up_columns(count, where, up_ref, xh, xl, vh, vl, er_ref, ei_ref, tables):
    plus_c, plus_s, minus_c, minus_s, polar_c, polar_s = tables
    left = iota((8, NB), 0) >= 3

    def columns(table, start):
        main = table[pl.ds(start + 8, F2), :]
        edge = jnp.where(left, table[pl.ds(start, 8), :], table[pl.ds(start + 97, 8), :])
        return jnp.concatenate([main, edge], axis=0)

    def two_rows(k, carry):
        n = where(k)
        for c in range(4):
            outs = []
            for h in range(2):
                t = 2 * n + h
                high = jnp.concatenate([xh[c, t], xh[c + 4, t]], axis=1)
                low = jnp.concatenate([xl[c, t], xl[c + 4, t]], axis=1)
                rhs = jnp.concatenate([high, low, high], axis=0)
                outs.append(jnp.dot(up_ref[...], rhs, preferred_element_type=F32))
            at = pl.ds(pl.multiple_of(16 * n, 16), 16)
            for g in range(12):
                rows = slice(8 * g, 8 * g + 8)
                hi, lo = halves(jnp.concatenate([outs[0][rows], outs[1][rows]], axis=0))
                vh[g, c, at, :] = hi
                vl[g, c, at, :] = lo
        for extra in range(6):
            r = jnp.minimum(6 * n + extra, ROWS - 1)
            e = times(columns(plus_c, r), columns(plus_s, r), columns(minus_c, 33 - r), columns(minus_s, 33 - r))
            e = times(*e, polar_c[pl.ds(r, 1), :], polar_s[pl.ds(r, 1), :])
            er_ref[r], ei_ref[r] = e
        return carry

    lax.fori_loop(0, count, two_rows, 0)


def up_blocks(numbers, theta_refs, z_ref, vh, vl, er_ref, ei_ref):
    keeps = [first_of_pair(m) for m in range(4)]

    def group(g, carry):
        rows = pl.ds(pl.multiple_of(8 * g, 8), 8)
        for number in numbers:
            first, last, t_first, t_last, tiles = BLOCKS[number]
            matrix = theta_refs[number]
            for c in range(4):
                part = slice(8 * t_first, 8 * t_last)
                high = vh[g, c, part, :]
                rhs = jnp.concatenate([high, vl[g, c, part, :], high], axis=0)
                v = jnp.dot(matrix[...], rhs, preferred_element_type=F32)
                for tile, start in tiles:
                    count = min(8, last - start) // 2
                    pairs = ([], [])
                    for m in range(count):
                        found = []
                        for p in (start + 2 * m, start + 2 * m + 1):
                            here = slice(8 * (p - first), 8 * (p - first) + 8)
                            e = er_ref[p + 6, rows, :], ei_ref[p + 6, rows, :]
                            found.append(times(v[here, 0:NB], v[here, NB : 2 * NB], *e))
                        for h in range(2):
                            pairs[h].append(merge(keeps[m], found[0][h], found[1][h], 64))
                    for h in range(2):
                        z_ref[tile, c + 4 * h, rows, :] = merge_tile(pairs[h], count)
        return carry

    lax.fori_loop(0, 12, group, 0, unroll=4)


def neighbours():
    theta, phi = lax.axis_index("theta"), lax.axis_index("phi")
    last = lax.axis_size("theta") - 1
    ring = lax.axis_size("phi")
    right = lax.rem(phi + 1, ring)
    left = lax.rem(phi + ring - 1, ring)
    out = []
    for dt in (-1, 0, 1):
        for df, column in ((-1, left), (0, phi), (1, right)):
            if dt == 0 and df == 0:
                continue
            has = None if dt == 0 else (theta > 0 if dt < 0 else theta < last)
            out.append((dt, df, has, (theta + dt, column)))
    return out


def guarded(has, do):
    if has is None:
        do()
    else:
        pl.when(has)(do)


def greet(around):
    barrier = pltpu.get_barrier_semaphore()
    for dt, df, has, device in around:
        def signal(device=device):
            pl.semaphore_signal(barrier, inc=1, device_id=device, device_id_type=MESH)

        guarded(has, signal)


def met(around):
    barrier = pltpu.get_barrier_semaphore()
    inside = around[0][2] & around[-1][2]

    @pl.when(inside)
    def _():
        pl.semaphore_wait(barrier, 8)

    @pl.when(jnp.logical_not(inside))
    def _():
        pl.semaphore_wait(barrier, 5)


def exchange(around, wanted, source, landing, send_sem, recv_sem):
    for n, (dt, df, has, device) in enumerate(around):
        if wanted(dt):
            copy = pltpu.make_async_remote_copy(
                src_ref=source(dt, df),
                dst_ref=landing[(-dt, -df)],
                send_sem=send_sem.at[n],
                recv_sem=recv_sem.at[7 - n],
                device_id=device,
                device_id_type=MESH,
            )
            guarded(has, copy.start)


def finish(around, wanted, source, landing, send_sem, recv_sem):
    for n, (dt, df, has, device) in enumerate(around):
        if not wanted(dt):
            continue
        copy = pltpu.make_async_remote_copy(
            src_ref=source(dt, df),
            dst_ref=landing[(dt, df)],
            send_sem=send_sem.at[n],
            recv_sem=recv_sem.at[n],
            device_id=device,
            device_id_type=MESH,
        )
        guarded(has, copy.wait)


STEP = 96


def child_setup(src_ref, kind_ref, hot_s, hot_k):
    row = lax.rem(iota((2 * NB, NB), 0), NB)
    for l in range(LIST):
        cut = slice(l * NB, l * NB + NB)
        hot_s[:, cut] = flags(row == src_ref[l : l + 1, :])
        hot_k[:, cut] = flags(row == kind_ref[l : l + 1, :])


def child_steps(low, high, x_ref, t_ref, o_ref, hot_s, hot_k, lx, lt):
    def step(g, carry):
        cut = pl.ds(2 * g, 2)
        for c in range(8):
            hi, lo = halves(x_ref[c, cut].reshape(STEP, NB))
            at = slice((2 * (c % 4) + c // 4) * STEP, (2 * (c % 4) + c // 4 + 1) * STEP)
            lx[at, 0:NB] = hi
            lx[at, NB : 2 * NB] = lo
        for c in range(2):
            hi, lo = halves(t_ref[c, cut].reshape(STEP, NB))
            lt[c * STEP : (c + 1) * STEP, 0:NB] = hi
            lt[c * STEP : (c + 1) * STEP, NB : 2 * NB] = lo
        total = [None] * 8
        for pair in range(LIST // 2):
            both = slice(pair * 2 * NB, (pair + 1) * 2 * NB)
            tt = jnp.dot(lt[...], hot_k[:, both], preferred_element_type=F32)
            for c in range(4):
                xx = jnp.dot(lx[2 * c * STEP : (2 * c + 2) * STEP, :], hot_s[:, both], preferred_element_type=F32)
                found = []
                for h in range(2):
                    one = slice(h * NB, h * NB + NB)
                    found.append(times(xx[:STEP, one], xx[STEP:, one], tt[:STEP, one], tt[STEP:, one]))
                for h in range(2):
                    value = (found[0][h] + found[1][h]).reshape(2, F1, NB)
                    if pair == 0:
                        o_ref[c + 4 * h, cut] = value
                    else:
                        o_ref[c + 4 * h, cut] += value
        return carry

    lax.fori_loop(low, high, step, 0)


def up_source(z_ref):
    def source(dt, df):
        if dt == 0:
            return z_ref.at[0:3, :, F2:QX, :]
        tile = 3 if dt < 0 else 4
        return z_ref.at[tile, :, 0:F2, :] if df == 0 else z_ref.at[tile, :, F2:QX, :]

    return source


def up_join(z_ref, tile, left, right):
    sub = iota((8, NB), 0)
    z_ref[tile, :, 0:8, :] += jnp.where((sub >= 1) & (sub <= 3), pltpu.roll(left, 1, 1), 0.0)
    z_ref[tile, :, F2 - 8 : F2, :] += jnp.where(sub >= 3, right, 0.0)


def up_join_outer(around, z_ref, landing):
    for side, has, tile in ((-1, around[0][2], 0), (1, around[-1][2], 2)):

        @pl.when(has)
        def _(side=side, tile=tile):
            z_ref[tile, :, 0:F2, :] += landing[(side, 0)][...]
            up_join(z_ref, tile, landing[(side, -1)][...], landing[(side, 1)][...])


def parent_setup(src_ref, kind_ref, hot_x, hot_t):
    row = iota((NB, NB), 0)
    for jj in range(4):
        keep = first_of_pair(jj)
        slot0, slot1 = REVERSED[2 * jj], REVERSED[2 * jj + 1]
        late_slot = jnp.where(keep, 16 * slot0, 16 * slot1)
        late = row == kind_ref[1:2, :]
        for half in range(2):
            cut = slice(half * NB, half * NB + NB)
            hot_x[jj, cut, 0:NB] = flags(row == src_ref[0:1, :] + 16 * slot0)
            hot_x[jj, cut, NB : 2 * NB] = flags(row == src_ref[0:1, :] + 16 * slot1)
            hot_x[jj, cut, 2 * NB : 3 * NB] = flags(row == src_ref[1:2, :] + late_slot)
            early = flags(row == kind_ref[0:1, :])
            hot_t[jj, 0, cut, 0:NB] = early
            hot_t[jj, 1, cut, 0:NB] = early
            hot_t[jj, 0, cut, NB : 2 * NB] = flags(late & keep)
            hot_t[jj, 1, cut, NB : 2 * NB] = flags(late & jnp.logical_not(keep))


def parent_rows(tiles, z_ref, t_ref, hot_x, hot_t, lx, lt, sums):
    lane = iota((1, NB), 1)
    halfway = [lax.rem(lane + 128 - 16 * q, 64) < 32 for q in range(2)]
    keeps = [first_of_pair(jj) for jj in range(4)]
    for tile in tiles:
        for c in range(8):
            hi, lo = halves(z_ref[tile, c, 0:F2, :])
            at = slice((2 * (c % 4) + c // 4) * F2, (2 * (c % 4) + c // 4 + 1) * F2)
            lx[tile, at, 0:NB] = hi
            lx[tile, at, NB : 2 * NB] = lo

    def quad(tile, q):
        tables = []
        for m in range(2):
            jj = 2 * q + m
            for r in range(2):
                for c in range(2):
                    hi, lo = halves(t_ref[c, jnp.minimum(8 * tile + 2 * jj + r, T2 - 1)])
                    lt[m, r, c * F2 : (c + 1) * F2, 0:NB] = hi
                    lt[m, r, c * F2 : (c + 1) * F2, NB : 2 * NB] = lo
            t0 = jnp.dot(lt[m, 0], hot_t[jj, 0], preferred_element_type=F32)
            t1 = jnp.dot(lt[m, 1], hot_t[jj, 1], preferred_element_type=F32)
            tables.append([t0[:, 0:NB], t1[:, 0:NB], t0[:, NB : 2 * NB] + t1[:, NB : 2 * NB]])
        for c in range(4):
            pairs = ([], [])
            for m in range(2):
                jj, tt = 2 * q + m, tables[m]
                xx = jnp.dot(lx[tile, 2 * c * F2 : (2 * c + 2) * F2, :], hot_x[jj], preferred_element_type=F32)
                parts = []
                for k in range(3):
                    one = slice(k * NB, k * NB + NB)
                    parts.append(times(xx[0:F2, one], xx[F2 : 2 * F2, one], tt[k][:F2], tt[k][F2:]))
                for h in range(2):
                    pairs[h].append(merge(keeps[jj], parts[0][h], parts[1][h], 64) + parts[2][h])
            for h in range(2):
                at = slice((c + 4 * h) * F2, (c + 4 * h + 1) * F2)
                sums[2 * tile + q, at, :] = merge(halfway[q], pairs[h][0], pairs[h][1], 96)

    def one_tile(k, carry):
        for q in range(2):
            quad(tiles[0] + 2 * k, q)
        return carry

    lax.fori_loop(0, len(tiles), one_tile, 0)


def parent_down(sums, theta_ref, phi_ref, w_ref, ld, rd):
    even = lax.rem(iota((1, NB), 1), 32) < 16
    for tile in range(3):
        hi, lo = halves(merge(even, sums[2 * tile], sums[2 * tile + 1], 112))
        ld[:, (3 * tile) * NB : (3 * tile + 1) * NB] = hi
        ld[:, (3 * tile + 1) * NB : (3 * tile + 2) * NB] = lo
        ld[:, (3 * tile + 2) * NB : (3 * tile + 3) * NB] = hi
    down = jnp.dot(ld[...], theta_ref[...], preferred_element_type=F32)
    for c in range(8):
        hi, lo = halves(down[c * F2 : (c + 1) * F2, :])
        cut = slice(c * 3 * NB, (c + 1) * 3 * NB)
        rd[0:F2, cut] = hi
        rd[96 : 96 + F2, cut] = lo
        rd[192 : 192 + F2, cut] = hi
    for c in range(8):
        cut = slice(c * 3 * NB, (c + 1) * 3 * NB)
        w_ref[c] = jnp.dot(phi_ref[...], rd[:, cut], preferred_element_type=F32)


def down_pack(w_ref, send_up, send_down):
    low = iota((F1 // 2, NB), 1) < 64
    for c in range(8):
        near = w_ref[c, 0 : F1 // 2, 2 * NB : 3 * NB]
        far = pltpu.roll(w_ref[c, F1 // 2 : F1, 2 * NB : 3 * NB], 64, 1)
        send_up[c] = jnp.where(low, near, far)
        send_down[c] = jnp.where(low, far, near)


def down_source(w_ref, send_up, send_down):
    def source(dt, df):
        if df == 0:
            return send_up if dt > 0 else send_down
        if dt == 0:
            return w_ref.at[:, F1:56, 0 : 2 * NB]
        return w_ref.at[:, F1:56, 2 * NB : 3 * NB]

    return source


def down_join(around, w_ref, wo_ref, landing):
    wo_ref[...] = w_ref[:, 0:F1, 0 : 2 * NB]
    sub = iota((8, 2 * NB), 0)
    wo_ref[:, 0:8, :] += jnp.where(sub < 3, landing[(0, -1)][...], 0.0)
    wo_ref[:, F1 - 8 : F1, :] += jnp.where(sub >= 5, landing[(0, 1)][...], 0.0)
    half = F1 // 2
    lane = iota((half, NB), 1)
    sub8, lane8 = iota((8, NB), 0), iota((8, NB), 1)

    @pl.when(around[0][2])
    def _():
        cut = slice(0, NB)
        for c in range(8):
            got = landing[(-1, 0)][c]
            wo_ref[c, 0:half, cut] += jnp.where(lane < 48, got, 0.0)
            wo_ref[c, half:F1, cut] += jnp.where(lane < 48, pltpu.roll(got, 64, 1), 0.0)
        wo_ref[:, 0:8, cut] += jnp.where((lane8 < 48) & (sub8 < 3), landing[(-1, -1)][...], 0.0)
        wo_ref[:, F1 - 8 : F1, cut] += jnp.where((lane8 < 48) & (sub8 >= 5), landing[(-1, 1)][...], 0.0)

    @pl.when(around[-1][2])
    def _():
        cut = slice(NB, 2 * NB)
        keep, keep8 = (lane >= 16) & (lane < 64), (lane8 >= 16) & (lane8 < 64)
        for c in range(8):
            got = landing[(1, 0)][c]
            wo_ref[c, 0:half, cut] += jnp.where(keep, pltpu.roll(got, 64, 1), 0.0)
            wo_ref[c, half:F1, cut] += jnp.where(keep, got, 0.0)
        wo_ref[:, 0:8, cut] += jnp.where(keep8 & (sub8 < 3), pltpu.roll(landing[(1, -1)][...], 64, 2), 0.0)
        wo_ref[:, F1 - 8 : F1, cut] += jnp.where(keep8 & (sub8 >= 5), pltpu.roll(landing[(1, 1)][...], 64, 2), 0.0)


EARLY = 3


def main_kernel(
    index_ref, table_ref, x_far, tc_far, tp_far, theta_far, up_ref, ta_ref, tb_ref, tc2_ref, td_ref, phi_ref, wo_ref, local_far, *scratch
):
    up_land, down_land, up_sems, down_sems = scratch[0:8], scratch[8:16], scratch[16:18], scratch[18:20]
    z_ref, lhs, order, xh, xl, vh, vl, er_ref, ei_ref = scratch[20:29]
    tables = views(table_ref, UP_ROWS)
    hot_s, hot_k, lx, lt = scratch[29:33]
    hot_x, hot_t, plx, plt, sums, ld, rd, w_ref = scratch[33:41]
    x_ref, tc_ref, tp_ref, theta_ref, local_ref, send_up, send_down, load_sem, store_sem = scratch[41:50]
    loads = [
        pltpu.make_async_copy(far, near, load_sem.at[n])
        for n, (far, near) in enumerate(
            ((x_far, x_ref), (tc_far, tc_ref), (tp_far, tp_ref), (theta_far, theta_ref))
        )
    ]
    stores = [
        pltpu.make_async_copy(local_ref.at[:, rows], local_far.at[:, rows], store_sem.at[n])
        for n, rows in enumerate((slice(0, 2 * EARLY), slice(2 * EARLY, T1)))
    ]
    for load in loads:
        load.start()
    keys = [(-1, 0), (1, 0), (0, -1), (0, 1), (-1, -1), (-1, 1), (1, -1), (1, 1)]
    up_landing, down_landing = dict(zip(keys, up_land)), dict(zip(keys, down_land))
    around = neighbours()
    greet(around)
    up_turn(index_ref[0:NB, :], loads[0], x_ref, lhs, order, xh, xl)
    column_refs = (up_ref, xh, xl, vh, vl, er_ref, ei_ref, tables)
    up_columns(4, lambda k: k + 2 * (k // 2), *column_refs)
    shared = ((ta_ref, tb_ref, tc2_ref, td_ref), z_ref, vh, vl, er_ref, ei_ref)
    up_blocks((0, 1), *shared)
    met(around)
    source = up_source(z_ref)
    exchange(around, lambda dt: dt != 0, source, up_landing, *up_sems)
    up_columns(2, lambda k: k + 2, *column_refs)
    up_blocks((2, 3), *shared)
    exchange(around, lambda dt: dt == 0, source, up_landing, *up_sems)
    child_setup(index_ref.at[NB + 8 : NB + 24], index_ref.at[NB + 24 : NB + 40], hot_s, hot_k)
    children = (x_ref, tc_ref, local_ref, hot_s, hot_k, lx, lt)
    rd[...] = jnp.zeros_like(rd)
    parent_setup(index_ref.at[NB + 20 : NB + 22], index_ref.at[NB + 36 : NB + 38], hot_x, hot_t)
    loads[1].wait()
    child_steps(0, EARLY, *children)
    stores[0].start()
    finish(around, lambda dt: dt == 0, source, up_landing, *up_sems)
    for tile in range(3):
        up_join(z_ref, tile, up_landing[(0, -1)][tile], up_landing[(0, 1)][tile])
    loads[2].wait()
    parent = (z_ref, tp_ref, hot_x, hot_t, plx, plt, sums)
    parent_rows((1,), *parent)
    finish(around, lambda dt: dt != 0, source, up_landing, *up_sems)
    up_join_outer(around, z_ref, up_landing)
    parent_rows((0, 2), *parent)
    loads[3].wait()
    parent_down(sums, theta_ref, phi_ref, w_ref, ld, rd)
    down_pack(w_ref, send_up, send_down)
    source = down_source(w_ref, send_up, send_down)
    exchange(around, lambda dt: True, source, down_landing, *down_sems)
    child_steps(EARLY, T1 // 2, *children)
    stores[1].start()
    finish(around, lambda dt: True, source, down_landing, *down_sems)
    down_join(around, w_ref, wo_ref, down_landing)
    for store in stores:
        store.wait()


FINAL = 2


def final_kernel(slot_ref, table_ref, w_ref, local_ref, o_ref, lw, spread):
    plus_c, plus_s, minus_c, minus_s, polar_c, polar_s = views(table_ref, DOWN_ROWS)

    @pl.when(pl.program_id(0) == 0)
    def _():
        row = iota((NB, NB), 0)
        parent = lax.rem(jnp.broadcast_to(slot_ref[...], (NB, NB)), 16)
        for j in range(8):
            block = flags(row == parent + 16 * j)
            spread[j, 0:NB, :] = block
            spread[j, NB : 2 * NB, :] = block
        for tile in range(2):
            for c in range(8):
                hi, lo = halves(w_ref[c, :, tile * NB : (tile + 1) * NB])
                lw[tile, c * F1 : (c + 1) * F1, 0:NB] = hi
                lw[tile, c * F1 : (c + 1) * F1, NB : 2 * NB] = lo

    for n in range(FINAL):
        t = pl.program_id(0) * FINAL + n
        wide = jnp.dot(lw[t // 8], spread[lax.rem(t, 8)], preferred_element_type=F32)
        er, ei = times(
            plus_c[pl.ds(t, F1), :],
            plus_s[pl.ds(t, F1), :],
            minus_c[pl.ds(11 - t, F1), :],
            minus_s[pl.ds(11 - t, F1), :],
        )
        er, ei = times(er, ei, polar_c[pl.ds(t, 1), :], polar_s[pl.ds(t, 1), :])
        for c in range(4):
            u, v = wide[c * F1 : (c + 1) * F1], wide[(c + 4) * F1 : (c + 5) * F1]
            re, im = times(u, v, er, -ei)
            o_ref[c, n] = re + local_ref[c, n]
            o_ref[c + 4, n] = im + local_ref[c + 4, n]


def shape(*dims):
    return jax.ShapeDtypeStruct(dims, F32)


def landing_scratch(column, row, corner):
    return [pltpu.VMEM(column, F32)] * 2 + [pltpu.VMEM(row, F32)] * 2 + [pltpu.VMEM(corner, F32)] * 4


def per_device(child_out, child_slot, sources_child, kinds_child, table_child, sources_parent, kinds_parent, table_parent):
    slot_row = child_slot.reshape(1, NB)
    params = dict(vmem_limit_bytes=60 * 1024 * 1024)
    index, up_table, down_table = pl.pallas_call(
        index_kernel,
        out_shape=(
            jax.ShapeDtypeStruct((INDEX_ROWS, NB), jnp.int32),
            shape(table_rows(UP_ROWS)[1], NB),
            shape(table_rows(DOWN_ROWS)[1], NB),
        ),
        in_specs=[VM] * 5,
        out_specs=(VM, VM, VM),
        scratch_shapes=[pltpu.VMEM((NB, NB), jnp.int32)],
        name="index",
    )(slot_row, sources_child.T, kinds_child.T, sources_parent, kinds_parent)

    wo, local = pl.pallas_call(
        main_kernel,
        out_shape=(shape(8, F1, 2 * NB), shape(8, T1, F1, NB)),
        in_specs=[VM] * 2 + [ANY] * 4 + [VM] * 6,
        out_specs=(VM, ANY),
        scratch_shapes=landing_scratch((8, F2, NB), (3, 8, 8, NB), (8, 8, NB))
        + landing_scratch((8, F1 // 2, NB), (8, 8, 2 * NB), (8, 8, NB))
        + [pltpu.SemaphoreType.DMA((8,))] * 4
        + [
            pltpu.VMEM((5, 8, QX, NB), F32),
            pltpu.VMEM((T1 * F1, 2 * NB), BF16),
            pltpu.VMEM((2 * NB, 2 * NB), BF16),
            pltpu.VMEM((8, T1, F1, NB), BF16),
            pltpu.VMEM((8, T1, F1, NB), BF16),
            pltpu.VMEM((12, 4, 8 * T1, 2 * NB), BF16),
            pltpu.VMEM((12, 4, 8 * T1, 2 * NB), BF16),
            pltpu.VMEM((ROWS, QX, NB), F32),
            pltpu.VMEM((ROWS, QX, NB), F32),
        ]
        + [pltpu.VMEM((2 * NB, LIST * NB), BF16)] * 2
        + [pltpu.VMEM((8 * STEP, 2 * NB), BF16), pltpu.VMEM((2 * STEP, 2 * NB), BF16)]
        + [
            pltpu.VMEM((4, 2 * NB, 3 * NB), BF16),
            pltpu.VMEM((4, 2, 2 * NB, 2 * NB), BF16),
            pltpu.VMEM((3, 8 * F2, 2 * NB), BF16),
            pltpu.VMEM((2, 2, 2 * F2, 2 * NB), BF16),
            pltpu.VMEM((6, 8 * F2, NB), F32),
            pltpu.VMEM((8 * F2, 9 * NB), BF16),
            pltpu.VMEM((288, 8 * 3 * NB), BF16),
            pltpu.VMEM((8, 56, 3 * NB), F32),
            pltpu.VMEM((8, T1, F1, NB), F32),
            pltpu.VMEM((2, T1, F1, NB), F32),
            pltpu.VMEM((2, T2, F2, NB), F32),
            pltpu.VMEM((9 * NB, 3 * NB), BF16),
            pltpu.VMEM((8, T1, F1, NB), F32),
            pltpu.VMEM((8, F1 // 2, NB), F32),
            pltpu.VMEM((8, F1 // 2, NB), F32),
            pltpu.SemaphoreType.DMA((4,)),
            pltpu.SemaphoreType.DMA((2,)),
        ],
        compiler_params=pltpu.CompilerParams(collective_id=0, has_side_effects=True, **params),
        name="main",
    )(
        index,
        up_table,
        child_out,
        table_child,
        table_parent,
        jnp.asarray(theta_down()),
        jnp.asarray(phi_up()),
        *[jnp.asarray(theta_up(*block[:4])) for block in BLOCKS],
        jnp.asarray(phi_down()),
    )

    return pl.pallas_call(
        final_kernel,
        grid=(T1 // FINAL,),
        out_shape=shape(8, T1, F1, NB),
        in_specs=[
            pl.BlockSpec((1, NB), lambda n: (0, 0)),
            pl.BlockSpec((table_rows(DOWN_ROWS)[1], NB), lambda n: (0, 0)),
            pl.BlockSpec((8, F1, 2 * NB), lambda n: (0, 0, 0)),
            pl.BlockSpec((8, FINAL, F1, NB), lambda n: (0, n, 0, 0)),
        ],
        out_specs=pl.BlockSpec((8, FINAL, F1, NB), lambda n: (0, n, 0, 0)),
        scratch_shapes=[pltpu.VMEM((2, 8 * F1, 2 * NB), BF16), pltpu.VMEM((8, 2 * NB, NB), BF16)],
        compiler_params=pltpu.CompilerParams(**params),
        name="final",
    )(slot_row, down_table, wo, local)


def solution(mesh):
    block = P(None, "theta", "phi", None)
    return jax.shard_map(
        per_device,
        mesh=mesh,
        in_specs=(block, P(), P(), P(), block, P(), P(), block),
        out_specs=block,
        check_vma=False,
    )
```

```python
import functools
import math

import jax
import jax.numpy as jnp
import numpy as np
from jax import lax
from jax.experimental import pallas as pl
from jax.experimental.pallas import tpu as pltpu
from jax.sharding import PartitionSpec as P

TH1, PH1, TH2, PH2 = 192, 384, 352, 704
BAND1 = 180
LIST = 12
T1, F1, T2, F2 = 12, 48, 22, 88
QX = 96
NB = 128
ROWS = 34
WAVE = BAND1 / (2.0 * math.sqrt(3.0))
REVERSED = (0, 4, 2, 6, 1, 5, 3, 7)
F32, BF16 = jnp.float32, jnp.bfloat16
MESH = pl.DeviceIdType.MESH
VM = pl.BlockSpec(memory_space=pltpu.VMEM)
ANY = pl.BlockSpec(memory_space=pl.ANY)


def stencil(count_out, count_in, centered, row_out):
    if centered:
        numerator = (2 * row_out + 1) * count_in - count_out
    else:
        numerator = 2 * row_out * count_in
    denominator = 2 * count_out
    base = numerator // denominator
    fraction = (numerator - base * denominator) / denominator
    weights = []
    for a in range(-2, 4):
        weight = 1.0
        for b in range(-2, 4):
            if b != a:
                weight = weight * (fraction - b) / (a - b)
        weights.append(weight)
    return base, weights


def as_halves(matrix):
    matrix = np.asarray(matrix, np.float32)
    high = matrix.astype(BF16)
    low = (matrix - high.astype(np.float32)).astype(BF16)
    return high, low


def parent_columns():
    return list(range(F2)) + [89, 90, 91, -5, -4, -3, -2, -1]


def child_columns():
    return list(range(F1)) + [48, 49, 50, None, None, -3, -2, -1]


def theta_up(first, last, t_first, t_last):
    matrix = np.zeros((last - first, t_last - t_first))
    for p in range(first, last):
        base, weights = stencil(TH2, TH1, True, p)
        for m in range(6):
            t = base - 2 + m
            if 0 <= t < T1:
                matrix[p - first, t - t_first] += weights[m]
    high, low = as_halves(np.kron(matrix, np.eye(8)))
    return np.concatenate([high, high, low], axis=1)


BLOCKS = (
    (-6, 0, 0, 4, ((3, -6),)),
    (22, 28, 8, 12, ((4, 22),)),
    (0, 8, 0, 8, ((0, 0),)),
    (8, 22, 2, 12, ((1, 8), (2, 16))),
)


def phi_up():
    matrix = np.zeros((QX, F1))
    for row, q in enumerate(parent_columns()):
        base, weights = stencil(PH2, PH1, False, q)
        for m in range(6):
            f = base - 2 + m
            if 0 <= f < F1:
                matrix[row, f] += weights[m]
    high, low = as_halves(matrix)
    return np.concatenate([high, high, low], axis=1)


def phi_down():
    matrix = np.zeros((56, 96))
    where = {f: row for row, f in enumerate(child_columns()) if f is not None}
    for q in range(F2):
        base, weights = stencil(PH2, PH1, False, q)
        for m in range(6):
            if weights[m] != 0.0:
                matrix[where[base - 2 + m], q] += weights[m]
    high, low = as_halves(matrix)
    return np.concatenate([high, high, low], axis=1)


def theta_down():
    slots = {}
    for t in range(T1):
        slots[t] = t
    for t in range(3):
        slots[12 + t] = 16 + t
        slots[t - 3] = 21 + t
    matrix = np.zeros((24, 24))
    for p in range(T2):
        base, weights = stencil(TH2, TH1, True, p)
        for m in range(6):
            matrix[p, slots[base - 2 + m]] += weights[m]
    matrix = matrix[[8 * (g // 8) + REVERSED[g % 8] for g in range(24)]]
    big = np.kron(matrix, np.eye(16))
    high, low = as_halves(big)
    parts = []
    for tile in range(3):
        cut = slice(128 * tile, 128 * tile + 128)
        parts += [high[cut], high[cut], low[cut]]
    return np.concatenate(parts, axis=0)


def halves(x):
    high = x.astype(BF16)
    return high, (x - high.astype(F32)).astype(BF16)


def iota(shape, dim):
    return lax.broadcasted_iota(jnp.int32, shape, dim)


def flags(condition):
    return jnp.where(condition, 1.0, 0.0).astype(BF16)


def ring_phase(index, shift, period):
    value = index - shift
    value = jnp.where(value >= period, value - period, value)
    value = jnp.where(value >= period, value - period, value)
    value = jnp.where(value < 0, value + period, value)
    value = jnp.where(value < 0, value + period, value)
    angle = (value.astype(F32) + 0.5) * (2.0 * math.pi / period)
    phase = (WAVE / math.sqrt(2.0)) * jnp.sin(angle)
    return jnp.cos(phase), jnp.sin(phase)


def octant_shift(octant, eighth):
    east = octant % 2
    north = (octant // 2) % 2
    quarter = jnp.where(east == 1, eighth, 3 * eighth)
    return jnp.where(north == 1, quarter, -quarter)


UP_ROWS, DOWN_ROWS = (144, 40), (64, 16)


def table_rows(rows):
    starts = [0, rows[0], 2 * rows[0], 3 * rows[0], 4 * rows[0], 4 * rows[0] + rows[1]]
    return starts, 4 * rows[0] + 2 * rows[1]


def views(ref, rows):
    starts, end = table_rows(rows)
    return [ref.at[low:high] for low, high in zip(starts, starts[1:] + [end])]


def fill_phases(octant, o_ref, rows, first_plus, first_minus, polar_first, period):
    starts, end = table_rows(rows)
    lane = iota((8, NB), 1)
    shift = octant_shift(lane // 16, period // 8)
    sign = jnp.where(lane // 64 == 1, WAVE, -WAVE)
    for n in range(0, max(rows), 128):
        row = n + 8 * lax.rem(lane, 16) + iota((8, NB), 0)
        polar = (row + polar_first).astype(F32) + 0.5
        phase = sign * jnp.cos(polar * (2.0 * math.pi / period))
        packed = (
            *ring_phase(row + first_plus, shift, period),
            *ring_phase(-(row + first_minus), -shift, period),
            jnp.cos(phase),
            jnp.sin(phase),
        )
        for k in range(6):
            for j in range(min(16, (rows[k // 4] - n) // 8)):
                spread = jnp.take_along_axis(packed[k], octant * 16 + j, axis=1)
                o_ref[starts[k] + n + 8 * j : starts[k] + n + 8 * j + 8, :] = spread


def times(ar, ai, br, bi):
    return ar * br - ai * bi, ar * bi + ai * br


INDEX_ROWS = NB + 40


def index_kernel(slot_ref, sc_ref, kc_ref, sp_ref, kp_ref, o_ref, up_ref, down_ref, wide):
    theta, phi = lax.axis_index("theta"), lax.axis_index("phi")
    i0, k0 = theta * T2, phi * F2
    fill_phases(iota((8, NB), 1) // 16, up_ref, UP_ROWS, i0 + k0 - 14, k0 - i0 - 35, i0 - 6, PH2)
    t0, f0 = theta * T1, phi * F1
    octant = jnp.broadcast_to(slot_ref[...] // 16, (8, NB))
    fill_phases(octant, down_ref, DOWN_ROWS, t0 + f0, f0 - t0 - 11, t0, PH1)
    o_ref[0:NB, :] = jnp.broadcast_to(slot_ref[...], (NB, NB)).T
    o_ref[NB : NB + 8, :] = jnp.broadcast_to(slot_ref[...], (8, NB))
    lane, row = iota((16, NB), 1), iota((16, NB), 0)
    for n, ref in enumerate((sc_ref, kc_ref)):
        o_ref[NB + 8 + 16 * n : NB + 8 + LIST + 16 * n, :] = ref[...]
    wide[...] = jnp.zeros_like(wide)
    for n, ref in enumerate((sp_ref, kp_ref)):
        wide[0:16, 0:LIST] = ref[...]
        turned = wide[...].T[0:16].astype(F32)
        for step in (16, 32, 64):
            turned = turned + pltpu.roll(turned, step, 1)
        early = jnp.sum(jnp.where(row == lane // 16, turned, 0.0), axis=0, keepdims=True)
        late = jnp.sum(jnp.where(row == 8 + lax.rem(lane // 16, 4), turned, 0.0), axis=0, keepdims=True)
        o_ref[NB + 8 + 12 + 16 * n : NB + 9 + 12 + 16 * n, :] = early.astype(jnp.int32)
        o_ref[NB + 9 + 12 + 16 * n : NB + 10 + 12 + 16 * n, :] = late.astype(jnp.int32)


def first_of_pair(m):
    lane = lax.rem(iota((1, NB), 1) + (128 - 32 * lax.rem(m, 2) - 16 * (m // 2)), 128)
    return lane < 64


def merge(keep, a, b, shift):
    return jnp.where(keep, a, b) + pltpu.roll(jnp.where(keep, b, a), shift, 1)


def merge_tile(pairs, count):
    lane = iota((1, NB), 1)
    first, second = lax.rem(lane, 64) < 32, lax.rem(lane + 112, 64) < 32
    even = lax.rem(lane, 32) < 16
    late = pairs[3] if count == 4 else jnp.zeros_like(pairs[2])
    return merge(even, merge(first, pairs[0], pairs[1], 96), merge(second, pairs[2], late, 96), 112)


def up_turn(slot_col, load_x, x_ref, lhs, order, xh, xl):
    block = flags(iota((NB, NB), 1) == slot_col)
    order[...] = jnp.zeros_like(order)
    order[0:NB, 0:NB] = block
    order[NB : 2 * NB, NB : 2 * NB] = block

    load_x.wait()

    def turn(c, carry):
        hi, lo = halves(x_ref[c].reshape(T1 * F1, NB))
        lhs[:, 0:NB] = hi
        lhs[:, NB : 2 * NB] = lo
        out = jnp.dot(lhs[...], order[...], preferred_element_type=F32)
        xh[c] = out[:, 0:NB].astype(BF16).reshape(T1, F1, NB)
        xl[c] = out[:, NB : 2 * NB].astype(BF16).reshape(T1, F1, NB)
        return carry

    lax.fori_loop(0, 8, turn, 0)


def up_columns(count, where, up_ref, xh, xl, vh, vl, er_ref, ei_ref, tables):
    plus_c, plus_s, minus_c, minus_s, polar_c, polar_s = tables
    left = iota((8, NB), 0) >= 3

    def columns(table, start):
        main = table[pl.ds(start + 8, F2), :]
        edge = jnp.where(left, table[pl.ds(start, 8), :], table[pl.ds(start + 97, 8), :])
        return jnp.concatenate([main, edge], axis=0)

    def two_rows(k, carry):
        n = where(k)
        for c in range(4):
            outs = []
            for h in range(2):
                t = 2 * n + h
                high = jnp.concatenate([xh[c, t], xh[c + 4, t]], axis=1)
                low = jnp.concatenate([xl[c, t], xl[c + 4, t]], axis=1)
                rhs = jnp.concatenate([high, low, high], axis=0)
                outs.append(jnp.dot(up_ref[...], rhs, preferred_element_type=F32))
            at = pl.ds(pl.multiple_of(16 * n, 16), 16)
            for g in range(12):
                rows = slice(8 * g, 8 * g + 8)
                hi, lo = halves(jnp.concatenate([outs[0][rows], outs[1][rows]], axis=0))
                vh[g, c, at, :] = hi
                vl[g, c, at, :] = lo
        for extra in range(6):
            r = jnp.minimum(6 * n + extra, ROWS - 1)
            e = times(columns(plus_c, r), columns(plus_s, r), columns(minus_c, 33 - r), columns(minus_s, 33 - r))
            e = times(*e, polar_c[pl.ds(r, 1), :], polar_s[pl.ds(r, 1), :])
            er_ref[r], ei_ref[r] = e
        return carry

    lax.fori_loop(0, count, two_rows, 0)


def up_blocks(numbers, theta_refs, z_ref, vh, vl, er_ref, ei_ref):
    keeps = [first_of_pair(m) for m in range(4)]

    def group(g, carry):
        rows = pl.ds(pl.multiple_of(8 * g, 8), 8)
        for number in numbers:
            first, last, t_first, t_last, tiles = BLOCKS[number]
            matrix = theta_refs[number]
            for c in range(4):
                part = slice(8 * t_first, 8 * t_last)
                high = vh[g, c, part, :]
                rhs = jnp.concatenate([high, vl[g, c, part, :], high], axis=0)
                v = jnp.dot(matrix[...], rhs, preferred_element_type=F32)
                for tile, start in tiles:
                    count = min(8, last - start) // 2
                    pairs = ([], [])
                    for m in range(count):
                        found = []
                        for p in (start + 2 * m, start + 2 * m + 1):
                            here = slice(8 * (p - first), 8 * (p - first) + 8)
                            e = er_ref[p + 6, rows, :], ei_ref[p + 6, rows, :]
                            found.append(times(v[here, 0:NB], v[here, NB : 2 * NB], *e))
                        for h in range(2):
                            pairs[h].append(merge(keeps[m], found[0][h], found[1][h], 64))
                    for h in range(2):
                        z_ref[tile, c + 4 * h, rows, :] = merge_tile(pairs[h], count)
        return carry

    lax.fori_loop(0, 12, group, 0, unroll=4)


def neighbours():
    theta, phi = lax.axis_index("theta"), lax.axis_index("phi")
    last = lax.axis_size("theta") - 1
    ring = lax.axis_size("phi")
    right = lax.rem(phi + 1, ring)
    left = lax.rem(phi + ring - 1, ring)
    out = []
    for dt in (-1, 0, 1):
        for df, column in ((-1, left), (0, phi), (1, right)):
            if dt == 0 and df == 0:
                continue
            has = None if dt == 0 else (theta > 0 if dt < 0 else theta < last)
            out.append((dt, df, has, (theta + dt, column)))
    return out


def guarded(has, do):
    if has is None:
        do()
    else:
        pl.when(has)(do)


def greet(around):
    barrier = pltpu.get_barrier_semaphore()
    for dt, df, has, device in around:
        def signal(device=device):
            pl.semaphore_signal(barrier, inc=1, device_id=device, device_id_type=MESH)

        guarded(has, signal)


def met(around):
    barrier = pltpu.get_barrier_semaphore()
    inside = around[0][2] & around[-1][2]

    @pl.when(inside)
    def _():
        pl.semaphore_wait(barrier, 8)

    @pl.when(jnp.logical_not(inside))
    def _():
        pl.semaphore_wait(barrier, 5)


def exchange(around, wanted, source, landing, send_sem, recv_sem):
    for n, (dt, df, has, device) in enumerate(around):
        if wanted(dt):
            copy = pltpu.make_async_remote_copy(
                src_ref=source(dt, df),
                dst_ref=landing[(-dt, -df)],
                send_sem=send_sem.at[n],
                recv_sem=recv_sem.at[7 - n],
                device_id=device,
                device_id_type=MESH,
            )
            guarded(has, copy.start)


def finish(around, wanted, source, landing, send_sem, recv_sem):
    for n, (dt, df, has, device) in enumerate(around):
        if not wanted(dt):
            continue
        copy = pltpu.make_async_remote_copy(
            src_ref=source(dt, df),
            dst_ref=landing[(dt, df)],
            send_sem=send_sem.at[n],
            recv_sem=recv_sem.at[n],
            device_id=device,
            device_id_type=MESH,
        )
        guarded(has, copy.wait)


STEP = 96


def child_setup(src_ref, kind_ref, hot_s, hot_k):
    row = lax.rem(iota((2 * NB, NB), 0), NB)
    for l in range(LIST):
        cut = slice(l * NB, l * NB + NB)
        hot_s[:, cut] = flags(row == src_ref[l : l + 1, :])
        hot_k[:, cut] = flags(row == kind_ref[l : l + 1, :])


def child_steps(low, high, x_ref, t_ref, o_ref, hot_s, hot_k, lx, lt):
    def step(g, carry):
        cut = pl.ds(2 * g, 2)
        for c in range(8):
            hi, lo = halves(x_ref[c, cut].reshape(STEP, NB))
            at = slice((2 * (c % 4) + c // 4) * STEP, (2 * (c % 4) + c // 4 + 1) * STEP)
            lx[at, 0:NB] = hi
            lx[at, NB : 2 * NB] = lo
        for c in range(2):
            hi, lo = halves(t_ref[c, cut].reshape(STEP, NB))
            lt[c * STEP : (c + 1) * STEP, 0:NB] = hi
            lt[c * STEP : (c + 1) * STEP, NB : 2 * NB] = lo
        total = [None] * 8
        for pair in range(LIST // 2):
            both = slice(pair * 2 * NB, (pair + 1) * 2 * NB)
            tt = jnp.dot(lt[...], hot_k[:, both], preferred_element_type=F32)
            for c in range(4):
                xx = jnp.dot(lx[2 * c * STEP : (2 * c + 2) * STEP, :], hot_s[:, both], preferred_element_type=F32)
                found = []
                for h in range(2):
                    one = slice(h * NB, h * NB + NB)
                    found.append(times(xx[:STEP, one], xx[STEP:, one], tt[:STEP, one], tt[STEP:, one]))
                for h in range(2):
                    value = (found[0][h] + found[1][h]).reshape(2, F1, NB)
                    if pair == 0:
                        o_ref[c + 4 * h, cut] = value
                    else:
                        o_ref[c + 4 * h, cut] += value
        return carry

    lax.fori_loop(low, high, step, 0)


def pack_right(low, high):
    return jnp.where(iota(low.shape, 1) < 3, low, pltpu.roll(high, 3, 1))


def up_source(z_ref, right_outer, right_inner):
    def source(dt, df):
        if dt == 0:
            return right_inner if df > 0 else z_ref.at[0:3, :, F2:QX, :]
        tile = 3 if dt < 0 else 4
        if df == 0:
            return z_ref.at[tile, :, 0:F2, :]
        return right_outer.at[tile - 3] if df > 0 else z_ref.at[tile, :, F2:QX, :]

    return source


def up_join(z_ref, tile, left, right):
    keep = (iota((4, 8, NB), 1) >= 1) & (iota((4, 8, NB), 1) <= 3)
    z_ref[tile, 0:4, 0:8, :] += jnp.where(keep, pltpu.roll(left, 1, 1), 0.0)
    z_ref[tile, 4:8, 0:8, :] += jnp.where(keep, pltpu.roll(left, 6, 1), 0.0)
    z_ref[tile, :, F2 - 8 : F2, :] += jnp.where(iota((8, NB), 0) >= 3, right, 0.0)


def up_join_outer(around, z_ref, landing):
    for side, has, tile in ((-1, around[0][2], 0), (1, around[-1][2], 2)):

        @pl.when(has)
        def _(side=side, tile=tile):
            z_ref[tile, :, 0:F2, :] += landing[(side, 0)][...]
            up_join(z_ref, tile, landing[(side, -1)][...], landing[(side, 1)][...])


def parent_setup(src_ref, kind_ref, hot_x, hot_t):
    row = iota((NB, NB), 0)
    for jj in range(4):
        keep = first_of_pair(jj)
        slot0, slot1 = REVERSED[2 * jj], REVERSED[2 * jj + 1]
        late_slot = jnp.where(keep, 16 * slot0, 16 * slot1)
        late = row == kind_ref[1:2, :]
        for half in range(2):
            cut = slice(half * NB, half * NB + NB)
            hot_x[jj, cut, 0:NB] = flags(row == src_ref[0:1, :] + 16 * slot0)
            hot_x[jj, cut, NB : 2 * NB] = flags(row == src_ref[0:1, :] + 16 * slot1)
            hot_x[jj, cut, 2 * NB : 3 * NB] = flags(row == src_ref[1:2, :] + late_slot)
            early = flags(row == kind_ref[0:1, :])
            hot_t[jj, 0, cut, 0:NB] = early
            hot_t[jj, 1, cut, 0:NB] = early
            hot_t[jj, 0, cut, NB : 2 * NB] = flags(late & keep)
            hot_t[jj, 1, cut, NB : 2 * NB] = flags(late & jnp.logical_not(keep))


def parent_rows(tiles, z_ref, t_ref, hot_x, hot_t, lx, lt, sums):
    lane = iota((1, NB), 1)
    halfway = [lax.rem(lane + 128 - 16 * q, 64) < 32 for q in range(2)]
    keeps = [first_of_pair(jj) for jj in range(4)]
    for tile in tiles:
        for c in range(8):
            hi, lo = halves(z_ref[tile, c, 0:F2, :])
            at = slice((2 * (c % 4) + c // 4) * F2, (2 * (c % 4) + c // 4 + 1) * F2)
            lx[tile, at, 0:NB] = hi
            lx[tile, at, NB : 2 * NB] = lo

    def quad(tile, q):
        tables = []
        for m in range(2):
            jj = 2 * q + m
            for r in range(2):
                for c in range(2):
                    hi, lo = halves(t_ref[c, jnp.minimum(8 * tile + 2 * jj + r, T2 - 1)])
                    lt[m, r, c * F2 : (c + 1) * F2, 0:NB] = hi
                    lt[m, r, c * F2 : (c + 1) * F2, NB : 2 * NB] = lo
            t0 = jnp.dot(lt[m, 0], hot_t[jj, 0], preferred_element_type=F32)
            t1 = jnp.dot(lt[m, 1], hot_t[jj, 1], preferred_element_type=F32)
            tables.append([t0[:, 0:NB], t1[:, 0:NB], t0[:, NB : 2 * NB] + t1[:, NB : 2 * NB]])
        for c in range(4):
            pairs = ([], [])
            for m in range(2):
                jj, tt = 2 * q + m, tables[m]
                xx = jnp.dot(lx[tile, 2 * c * F2 : (2 * c + 2) * F2, :], hot_x[jj], preferred_element_type=F32)
                parts = []
                for k in range(3):
                    one = slice(k * NB, k * NB + NB)
                    parts.append(times(xx[0:F2, one], xx[F2 : 2 * F2, one], tt[k][:F2], tt[k][F2:]))
                for h in range(2):
                    pairs[h].append(merge(keeps[jj], parts[0][h], parts[1][h], 64) + parts[2][h])
            for h in range(2):
                at = slice((c + 4 * h) * F2, (c + 4 * h + 1) * F2)
                sums[2 * tile + q, at, :] = merge(halfway[q], pairs[h][0], pairs[h][1], 96)

    def one_tile(k, carry):
        for q in range(2):
            quad(tiles[0] + 2 * k, q)
        return carry

    lax.fori_loop(0, len(tiles), one_tile, 0)


def parent_down(sums, theta_ref, phi_ref, w_ref, ld, rd):
    even = lax.rem(iota((1, NB), 1), 32) < 16
    for tile in range(3):
        hi, lo = halves(merge(even, sums[2 * tile], sums[2 * tile + 1], 112))
        ld[:, (3 * tile) * NB : (3 * tile + 1) * NB] = hi
        ld[:, (3 * tile + 1) * NB : (3 * tile + 2) * NB] = lo
        ld[:, (3 * tile + 2) * NB : (3 * tile + 3) * NB] = hi
    down = jnp.dot(ld[...], theta_ref[...], preferred_element_type=F32)
    for c in range(8):
        hi, lo = halves(down[c * F2 : (c + 1) * F2, :])
        cut = slice(c * 3 * NB, (c + 1) * 3 * NB)
        rd[0:F2, cut] = hi
        rd[96 : 96 + F2, cut] = lo
        rd[192 : 192 + F2, cut] = hi
    for c in range(8):
        cut = slice(c * 3 * NB, (c + 1) * 3 * NB)
        w_ref[c] = jnp.dot(phi_ref[...], rd[:, cut], preferred_element_type=F32)


def down_pack(w_ref, send_up, send_down, send_right, send_left):
    near, far = w_ref[0:4, F1:56, :], w_ref[4:8, F1:56, :]
    send_right[...] = pack_right(near, far)
    send_left[...] = jnp.where(iota(near.shape, 1) >= 5, near, pltpu.roll(far, 5, 1))
    low = iota((F1 // 2, NB), 1) < 64
    for c in range(8):
        near = w_ref[c, 0 : F1 // 2, 2 * NB : 3 * NB]
        far = pltpu.roll(w_ref[c, F1 // 2 : F1, 2 * NB : 3 * NB], 64, 1)
        send_up[c] = jnp.where(low, near, far)
        send_down[c] = jnp.where(low, far, near)


def down_source(send_up, send_down, send_right, send_left):
    def source(dt, df):
        if df == 0:
            return send_up if dt > 0 else send_down
        edge = send_right if df > 0 else send_left
        return edge.at[:, :, 0 : 2 * NB] if dt == 0 else edge.at[:, :, 2 * NB : 3 * NB]

    return source


def down_edges(wo_ref, cut, inside, left, right):
    sub = iota(left.shape, 1)
    first, last = slice(0, 8), slice(F1 - 8, F1)
    wo_ref[0:4, first, cut] += jnp.where(inside & (sub < 3), left, 0.0)
    wo_ref[4:8, first, cut] += jnp.where(inside & (sub < 3), pltpu.roll(left, 5, 1), 0.0)
    wo_ref[0:4, last, cut] += jnp.where(inside & (sub >= 5), right, 0.0)
    wo_ref[4:8, last, cut] += jnp.where(inside & (sub >= 5), pltpu.roll(right, 3, 1), 0.0)


def down_join(around, w_ref, wo_ref, landing):
    wo_ref[...] = w_ref[:, 0:F1, 0 : 2 * NB]
    all_lanes = iota((4, 8, 2 * NB), 2) >= 0
    down_edges(wo_ref, slice(0, 2 * NB), all_lanes, landing[(0, -1)][...], landing[(0, 1)][...])
    half = F1 // 2
    lane, lane8 = iota((half, NB), 1), iota((4, 8, NB), 2)

    @pl.when(around[0][2])
    def _():
        cut = slice(0, NB)
        for c in range(8):
            got = landing[(-1, 0)][c]
            wo_ref[c, 0:half, cut] += jnp.where(lane < 48, got, 0.0)
            wo_ref[c, half:F1, cut] += jnp.where(lane < 48, pltpu.roll(got, 64, 1), 0.0)
        down_edges(wo_ref, cut, lane8 < 48, landing[(-1, -1)][...], landing[(-1, 1)][...])

    @pl.when(around[-1][2])
    def _():
        cut = slice(NB, 2 * NB)
        keep = (lane >= 16) & (lane < 64)
        for c in range(8):
            got = landing[(1, 0)][c]
            wo_ref[c, 0:half, cut] += jnp.where(keep, pltpu.roll(got, 64, 1), 0.0)
            wo_ref[c, half:F1, cut] += jnp.where(keep, got, 0.0)
        left, right = pltpu.roll(landing[(1, -1)][...], 64, 2), pltpu.roll(landing[(1, 1)][...], 64, 2)
        down_edges(wo_ref, cut, (lane8 >= 16) & (lane8 < 64), left, right)


EARLY = 4


def main_kernel(
    index_ref, table_ref, x_far, tc_far, tp_far, theta_far, up_ref, ta_ref, tb_ref, tc2_ref, td_ref, phi_ref, wo_ref, local_far, *scratch
):
    up_land, down_land, up_sems, down_sems = scratch[0:8], scratch[8:16], scratch[16:18], scratch[18:20]
    z_ref, lhs, order, xh, xl, vh, vl, er_ref, ei_ref = scratch[20:29]
    tables = views(table_ref, UP_ROWS)
    hot_s, hot_k, lx, lt = scratch[29:33]
    hot_x, hot_t, plx, plt, sums, ld, rd, w_ref = scratch[33:41]
    x_ref, tc_ref, tp_ref, theta_ref, local_ref, send_up, send_down, load_sem, store_sem = scratch[41:50]
    right_outer, right_inner, send_right, send_left = scratch[50:54]
    loads = [
        pltpu.make_async_copy(far, near, load_sem.at[n])
        for n, (far, near) in enumerate(
            ((x_far, x_ref), (tc_far, tc_ref), (tp_far, tp_ref), (theta_far, theta_ref))
        )
    ]
    stores = [
        pltpu.make_async_copy(local_ref.at[:, rows], local_far.at[:, rows], store_sem.at[n])
        for n, rows in enumerate((slice(0, 2 * EARLY), slice(2 * EARLY, T1)))
    ]
    for load in loads:
        load.start()
    keys = [(-1, 0), (1, 0), (0, -1), (0, 1), (-1, -1), (-1, 1), (1, -1), (1, 1)]
    up_landing, down_landing = dict(zip(keys, up_land)), dict(zip(keys, down_land))
    around = neighbours()
    greet(around)
    up_turn(index_ref[0:NB, :], loads[0], x_ref, lhs, order, xh, xl)
    column_refs = (up_ref, xh, xl, vh, vl, er_ref, ei_ref, tables)
    up_columns(4, lambda k: k + 2 * (k // 2), *column_refs)
    shared = ((ta_ref, tb_ref, tc2_ref, td_ref), z_ref, vh, vl, er_ref, ei_ref)
    up_blocks((0, 1), *shared)
    met(around)
    for n in range(2):
        right_outer[n] = pack_right(z_ref[3 + n, 0:4, F2:QX, :], z_ref[3 + n, 4:8, F2:QX, :])
    source = up_source(z_ref, right_outer, right_inner)
    exchange(around, lambda dt: dt != 0, source, up_landing, *up_sems)
    up_columns(2, lambda k: k + 2, *column_refs)
    up_blocks((2, 3), *shared)
    for n in range(3):
        right_inner[n] = pack_right(z_ref[n, 0:4, F2:QX, :], z_ref[n, 4:8, F2:QX, :])
    exchange(around, lambda dt: dt == 0, source, up_landing, *up_sems)
    child_setup(index_ref.at[NB + 8 : NB + 24], index_ref.at[NB + 24 : NB + 40], hot_s, hot_k)
    children = (x_ref, tc_ref, local_ref, hot_s, hot_k, lx, lt)
    rd[...] = jnp.zeros_like(rd)
    parent_setup(index_ref.at[NB + 20 : NB + 22], index_ref.at[NB + 36 : NB + 38], hot_x, hot_t)
    loads[1].wait()
    child_steps(0, EARLY, *children)
    stores[0].start()
    finish(around, lambda dt: dt == 0, source, up_landing, *up_sems)
    for tile in range(3):
        up_join(z_ref, tile, up_landing[(0, -1)][tile], up_landing[(0, 1)][tile])
    loads[2].wait()
    parent = (z_ref, tp_ref, hot_x, hot_t, plx, plt, sums)
    parent_rows((1,), *parent)
    finish(around, lambda dt: dt != 0, source, up_landing, *up_sems)
    up_join_outer(around, z_ref, up_landing)
    parent_rows((0, 2), *parent)
    loads[3].wait()
    parent_down(sums, theta_ref, phi_ref, w_ref, ld, rd)
    down_pack(w_ref, send_up, send_down, send_right, send_left)
    source = down_source(send_up, send_down, send_right, send_left)
    exchange(around, lambda dt: True, source, down_landing, *down_sems)
    child_steps(EARLY, T1 // 2, *children)
    stores[1].start()
    finish(around, lambda dt: True, source, down_landing, *down_sems)
    down_join(around, w_ref, wo_ref, down_landing)
    for store in stores:
        store.wait()


FINAL = 2


def final_kernel(slot_ref, table_ref, w_ref, local_far, o_far, lw, spread, local_ref, o_ref, load_sem, store_sem):
    parts = [slice(n * FINAL, n * FINAL + FINAL) for n in range(T1 // FINAL)]
    loads = [
        pltpu.make_async_copy(local_far.at[:, rows], local_ref.at[:, rows], load_sem.at[n])
        for n, rows in enumerate(parts)
    ]
    stores = [
        pltpu.make_async_copy(o_ref.at[:, rows], o_far.at[:, rows], store_sem.at[n])
        for n, rows in enumerate(parts)
    ]
    for load in loads:
        load.start()
    plus_c, plus_s, minus_c, minus_s, polar_c, polar_s = views(table_ref, DOWN_ROWS)

    row = iota((NB, NB), 0)
    parent = lax.rem(jnp.broadcast_to(slot_ref[...], (NB, NB)), 16)
    for j in range(8):
        block = flags(row == parent + 16 * j)
        spread[j, 0:NB, :] = block
        spread[j, NB : 2 * NB, :] = block
    for tile in range(2):
        for c in range(8):
            hi, lo = halves(w_ref[c, :, tile * NB : (tile + 1) * NB])
            lw[tile, c * F1 : (c + 1) * F1, 0:NB] = hi
            lw[tile, c * F1 : (c + 1) * F1, NB : 2 * NB] = lo

    def one_row(t):
        wide = jnp.dot(lw[t // 8], spread[t % 8], preferred_element_type=F32)
        er, ei = times(
            plus_c[pl.ds(t, F1), :],
            plus_s[pl.ds(t, F1), :],
            minus_c[pl.ds(11 - t, F1), :],
            minus_s[pl.ds(11 - t, F1), :],
        )
        er, ei = times(er, ei, polar_c[pl.ds(t, 1), :], polar_s[pl.ds(t, 1), :])
        for c in range(4):
            u, v = wide[c * F1 : (c + 1) * F1], wide[(c + 4) * F1 : (c + 5) * F1]
            re, im = times(u, v, er, -ei)
            o_ref[c, t] = re + local_ref[c, t]
            o_ref[c + 4, t] = im + local_ref[c + 4, t]

    for n in range(T1 // FINAL):
        loads[n].wait()
        for t in range(n * FINAL, n * FINAL + FINAL):
            one_row(t)
        stores[n].start()
    for store in stores:
        store.wait()


def shape(*dims):
    return jax.ShapeDtypeStruct(dims, F32)


def landing_scratch(outer, left, right, corner_left, corner_right):
    return [pltpu.VMEM(dims, F32) for dims in [outer] * 2 + [left, right] + [corner_left, corner_right] * 2]


def per_device(child_out, child_slot, sources_child, kinds_child, table_child, sources_parent, kinds_parent, table_parent):
    slot_row = child_slot.reshape(1, NB)
    params = dict(vmem_limit_bytes=60 * 1024 * 1024)
    index, up_table, down_table = pl.pallas_call(
        index_kernel,
        out_shape=(
            jax.ShapeDtypeStruct((INDEX_ROWS, NB), jnp.int32),
            shape(table_rows(UP_ROWS)[1], NB),
            shape(table_rows(DOWN_ROWS)[1], NB),
        ),
        in_specs=[VM] * 5,
        out_specs=(VM, VM, VM),
        scratch_shapes=[pltpu.VMEM((NB, NB), jnp.int32)],
        name="index",
    )(slot_row, sources_child.T, kinds_child.T, sources_parent, kinds_parent)

    wo, local = pl.pallas_call(
        main_kernel,
        out_shape=(shape(8, F1, 2 * NB), shape(8, T1, F1, NB)),
        in_specs=[VM] * 2 + [ANY] * 4 + [VM] * 6,
        out_specs=(VM, ANY),
        scratch_shapes=landing_scratch((8, F2, NB), (3, 4, 8, NB), (3, 8, 8, NB), (4, 8, NB), (8, 8, NB))
        + landing_scratch((8, F1 // 2, NB), (4, 8, 2 * NB), (4, 8, 2 * NB), (4, 8, NB), (4, 8, NB))
        + [pltpu.SemaphoreType.DMA((8,))] * 4
        + [
            pltpu.VMEM((5, 8, QX, NB), F32),
            pltpu.VMEM((T1 * F1, 2 * NB), BF16),
            pltpu.VMEM((2 * NB, 2 * NB), BF16),
            pltpu.VMEM((8, T1, F1, NB), BF16),
            pltpu.VMEM((8, T1, F1, NB), BF16),
            pltpu.VMEM((12, 4, 8 * T1, 2 * NB), BF16),
            pltpu.VMEM((12, 4, 8 * T1, 2 * NB), BF16),
            pltpu.VMEM((ROWS, QX, NB), F32),
            pltpu.VMEM((ROWS, QX, NB), F32),
        ]
        + [pltpu.VMEM((2 * NB, LIST * NB), BF16)] * 2
        + [pltpu.VMEM((8 * STEP, 2 * NB), BF16), pltpu.VMEM((2 * STEP, 2 * NB), BF16)]
        + [
            pltpu.VMEM((4, 2 * NB, 3 * NB), BF16),
            pltpu.VMEM((4, 2, 2 * NB, 2 * NB), BF16),
            pltpu.VMEM((3, 8 * F2, 2 * NB), BF16),
            pltpu.VMEM((2, 2, 2 * F2, 2 * NB), BF16),
            pltpu.VMEM((6, 8 * F2, NB), F32),
            pltpu.VMEM((8 * F2, 9 * NB), BF16),
            pltpu.VMEM((288, 8 * 3 * NB), BF16),
            pltpu.VMEM((8, 56, 3 * NB), F32),
            pltpu.VMEM((8, T1, F1, NB), F32),
            pltpu.VMEM((2, T1, F1, NB), F32),
            pltpu.VMEM((2, T2, F2, NB), F32),
            pltpu.VMEM((9 * NB, 3 * NB), BF16),
            pltpu.VMEM((8, T1, F1, NB), F32),
            pltpu.VMEM((8, F1 // 2, NB), F32),
            pltpu.VMEM((8, F1 // 2, NB), F32),
            pltpu.SemaphoreType.DMA((4,)),
            pltpu.SemaphoreType.DMA((2,)),
            pltpu.VMEM((2, 4, 8, NB), F32),
            pltpu.VMEM((3, 4, 8, NB), F32),
            pltpu.VMEM((4, 8, 3 * NB), F32),
            pltpu.VMEM((4, 8, 3 * NB), F32),
        ],
        compiler_params=pltpu.CompilerParams(collective_id=0, has_side_effects=True, **params),
        name="main",
    )(
        index,
        up_table,
        child_out,
        table_child,
        table_parent,
        jnp.asarray(theta_down()),
        jnp.asarray(phi_up()),
        *[jnp.asarray(theta_up(*block[:4])) for block in BLOCKS],
        jnp.asarray(phi_down()),
    )

    return pl.pallas_call(
        final_kernel,
        out_shape=shape(8, T1, F1, NB),
        in_specs=[VM, VM, VM, ANY],
        out_specs=ANY,
        scratch_shapes=[
            pltpu.VMEM((2, 8 * F1, 2 * NB), BF16),
            pltpu.VMEM((8, 2 * NB, NB), BF16),
            pltpu.VMEM((8, T1, F1, NB), F32),
            pltpu.VMEM((8, T1, F1, NB), F32),
            pltpu.SemaphoreType.DMA((T1 // FINAL,)),
            pltpu.SemaphoreType.DMA((T1 // FINAL,)),
        ],
        compiler_params=pltpu.CompilerParams(**params),
        name="final",
    )(slot_row, down_table, wo, local)


def solution(mesh):
    block = P(None, "theta", "phi", None)
    return jax.shard_map(
        per_device,
        mesh=mesh,
        in_specs=(block, P(), P(), P(), block, P(), P(), block),
        out_specs=block,
        check_vma=False,
    )
```

```python
import functools
import math

import jax
import jax.numpy as jnp
import numpy as np
from jax import lax
from jax.experimental import pallas as pl
from jax.experimental.pallas import tpu as pltpu
from jax.sharding import PartitionSpec as P

TH1, PH1, TH2, PH2 = 192, 384, 352, 704
BAND1 = 180
LIST = 12
T1, F1, T2, F2 = 12, 48, 22, 88
QX = 96
NB = 128
ROWS = 34
WAVE = BAND1 / (2.0 * math.sqrt(3.0))
REVERSED = (0, 4, 2, 6, 1, 5, 3, 7)
F32, BF16 = jnp.float32, jnp.bfloat16
MESH = pl.DeviceIdType.MESH
VM = pl.BlockSpec(memory_space=pltpu.VMEM)
ANY = pl.BlockSpec(memory_space=pl.ANY)


def stencil(count_out, count_in, centered, row_out):
    if centered:
        numerator = (2 * row_out + 1) * count_in - count_out
    else:
        numerator = 2 * row_out * count_in
    denominator = 2 * count_out
    base = numerator // denominator
    fraction = (numerator - base * denominator) / denominator
    weights = []
    for a in range(-2, 4):
        weight = 1.0
        for b in range(-2, 4):
            if b != a:
                weight = weight * (fraction - b) / (a - b)
        weights.append(weight)
    return base, weights


def as_halves(matrix):
    matrix = np.asarray(matrix, np.float32)
    high = matrix.astype(BF16)
    low = (matrix - high.astype(np.float32)).astype(BF16)
    return high, low


def parent_columns():
    return list(range(F2)) + [89, 90, 91, -5, -4, -3, -2, -1]


def child_columns():
    return list(range(F1)) + [48, 49, 50, None, None, -3, -2, -1]


def theta_up(first, last, t_first, t_last):
    matrix = np.zeros((last - first, t_last - t_first))
    for p in range(first, last):
        base, weights = stencil(TH2, TH1, True, p)
        for m in range(6):
            t = base - 2 + m
            if 0 <= t < T1:
                matrix[p - first, t - t_first] += weights[m]
    high, low = as_halves(np.kron(matrix, np.eye(8)))
    return np.concatenate([high, high, low], axis=1)


BLOCKS = (
    (-6, 0, 0, 4, ((3, -6),)),
    (22, 28, 8, 12, ((4, 22),)),
    (0, 8, 0, 8, ((0, 0),)),
    (8, 22, 2, 12, ((1, 8), (2, 16))),
)


def phi_up():
    matrix = np.zeros((QX, F1))
    for row, q in enumerate(parent_columns()):
        base, weights = stencil(PH2, PH1, False, q)
        for m in range(6):
            f = base - 2 + m
            if 0 <= f < F1:
                matrix[row, f] += weights[m]
    high, low = as_halves(matrix)
    return np.concatenate([high, high, low], axis=1)


def phi_down():
    matrix = np.zeros((56, 96))
    where = {f: row for row, f in enumerate(child_columns()) if f is not None}
    for q in range(F2):
        base, weights = stencil(PH2, PH1, False, q)
        for m in range(6):
            if weights[m] != 0.0:
                matrix[where[base - 2 + m], q] += weights[m]
    high, low = as_halves(matrix)
    return np.concatenate([high, high, low], axis=1)


def theta_down():
    slots = {}
    for t in range(T1):
        slots[t] = t
    for t in range(3):
        slots[12 + t] = 16 + t
        slots[t - 3] = 21 + t
    matrix = np.zeros((24, 24))
    for p in range(T2):
        base, weights = stencil(TH2, TH1, True, p)
        for m in range(6):
            matrix[p, slots[base - 2 + m]] += weights[m]
    matrix = matrix[[8 * (g // 8) + REVERSED[g % 8] for g in range(24)]]
    big = np.kron(matrix, np.eye(16))
    high, low = as_halves(big)
    parts = []
    for tile in range(3):
        cut = slice(128 * tile, 128 * tile + 128)
        parts += [high[cut], high[cut], low[cut]]
    return np.concatenate(parts, axis=0)


def halves(x):
    high = x.astype(BF16)
    return high, (x - high.astype(F32)).astype(BF16)


def iota(shape, dim):
    return lax.broadcasted_iota(jnp.int32, shape, dim)


def flags(condition):
    return jnp.where(condition, 1.0, 0.0).astype(BF16)


def ring_phase(index, shift, period):
    value = index - shift
    value = jnp.where(value >= period, value - period, value)
    value = jnp.where(value >= period, value - period, value)
    value = jnp.where(value < 0, value + period, value)
    value = jnp.where(value < 0, value + period, value)
    angle = (value.astype(F32) + 0.5) * (2.0 * math.pi / period)
    phase = (WAVE / math.sqrt(2.0)) * jnp.sin(angle)
    return jnp.cos(phase), jnp.sin(phase)


def octant_shift(octant, eighth):
    east = octant % 2
    north = (octant // 2) % 2
    quarter = jnp.where(east == 1, eighth, 3 * eighth)
    return jnp.where(north == 1, quarter, -quarter)


UP_ROWS, DOWN_ROWS = (144, 40), (64, 16)


def table_rows(rows):
    starts = [0, rows[0], 2 * rows[0], 3 * rows[0], 4 * rows[0], 4 * rows[0] + rows[1]]
    return starts, 4 * rows[0] + 2 * rows[1]


def views(ref, rows):
    starts, end = table_rows(rows)
    return [ref.at[low:high] for low, high in zip(starts, starts[1:] + [end])]


def fill_phases(octant, o_ref, rows, first_plus, first_minus, polar_first, period):
    starts, end = table_rows(rows)
    lane = iota((8, NB), 1)
    shift = octant_shift(lane // 16, period // 8)
    sign = jnp.where(lane // 64 == 1, WAVE, -WAVE)
    for n in range(0, max(rows), 128):
        row = n + 8 * lax.rem(lane, 16) + iota((8, NB), 0)
        polar = (row + polar_first).astype(F32) + 0.5
        phase = sign * jnp.cos(polar * (2.0 * math.pi / period))
        packed = (
            *ring_phase(row + first_plus, shift, period),
            *ring_phase(-(row + first_minus), -shift, period),
            jnp.cos(phase),
            jnp.sin(phase),
        )
        for k in range(6):
            for j in range(min(16, (rows[k // 4] - n) // 8)):
                spread = jnp.take_along_axis(packed[k], octant * 16 + j, axis=1)
                o_ref[starts[k] + n + 8 * j : starts[k] + n + 8 * j + 8, :] = spread


def times(ar, ai, br, bi):
    return ar * br - ai * bi, ar * bi + ai * br


INDEX_ROWS = NB + 40


def index_kernel(slot_ref, sc_ref, kc_ref, sp_ref, kp_ref, o_ref, up_ref, down_ref, wide):
    theta, phi = lax.axis_index("theta"), lax.axis_index("phi")
    i0, k0 = theta * T2, phi * F2
    fill_phases(iota((8, NB), 1) // 16, up_ref, UP_ROWS, i0 + k0 - 14, k0 - i0 - 35, i0 - 6, PH2)
    t0, f0 = theta * T1, phi * F1
    octant = jnp.broadcast_to(slot_ref[...] // 16, (8, NB))
    fill_phases(octant, down_ref, DOWN_ROWS, t0 + f0, f0 - t0 - 11, t0, PH1)
    o_ref[0:NB, :] = jnp.broadcast_to(slot_ref[...], (NB, NB)).T
    o_ref[NB : NB + 8, :] = jnp.broadcast_to(slot_ref[...], (8, NB))
    lane, row = iota((16, NB), 1), iota((16, NB), 0)
    for n, ref in enumerate((sc_ref, kc_ref)):
        o_ref[NB + 8 + 16 * n : NB + 8 + LIST + 16 * n, :] = ref[...]
    wide[...] = jnp.zeros_like(wide)
    for n, ref in enumerate((sp_ref, kp_ref)):
        wide[0:16, 0:LIST] = ref[...]
        turned = wide[...].T[0:16].astype(F32)
        for step in (16, 32, 64):
            turned = turned + pltpu.roll(turned, step, 1)
        early = jnp.sum(jnp.where(row == lane // 16, turned, 0.0), axis=0, keepdims=True)
        late = jnp.sum(jnp.where(row == 8 + lax.rem(lane // 16, 4), turned, 0.0), axis=0, keepdims=True)
        o_ref[NB + 8 + 12 + 16 * n : NB + 9 + 12 + 16 * n, :] = early.astype(jnp.int32)
        o_ref[NB + 9 + 12 + 16 * n : NB + 10 + 12 + 16 * n, :] = late.astype(jnp.int32)


def first_of_pair(m):
    lane = lax.rem(iota((1, NB), 1) + (128 - 32 * lax.rem(m, 2) - 16 * (m // 2)), 128)
    return lane < 64


def merge(keep, a, b, shift):
    return jnp.where(keep, a, b) + pltpu.roll(jnp.where(keep, b, a), shift, 1)


def merge_tile(pairs, count):
    lane = iota((1, NB), 1)
    first, second = lax.rem(lane, 64) < 32, lax.rem(lane + 112, 64) < 32
    even = lax.rem(lane, 32) < 16
    late = pairs[3] if count == 4 else jnp.zeros_like(pairs[2])
    return merge(even, merge(first, pairs[0], pairs[1], 96), merge(second, pairs[2], late, 96), 112)


def up_turn(slot_col, load_x, x_ref, lhs, order, xh, xl):
    block = flags(iota((NB, NB), 1) == slot_col)
    order[...] = jnp.zeros_like(order)
    order[0:NB, 0:NB] = block
    order[NB : 2 * NB, NB : 2 * NB] = block

    load_x.wait()

    def turn(c, carry):
        hi, lo = halves(x_ref[c].reshape(T1 * F1, NB))
        lhs[:, 0:NB] = hi
        lhs[:, NB : 2 * NB] = lo
        out = jnp.dot(lhs[...], order[...], preferred_element_type=F32)
        xh[c] = out[:, 0:NB].astype(BF16).reshape(T1, F1, NB)
        xl[c] = out[:, NB : 2 * NB].astype(BF16).reshape(T1, F1, NB)
        return carry

    lax.fori_loop(0, 8, turn, 0)


def up_columns(count, where, up_ref, xh, xl, vh, vl, er_ref, ei_ref, tables):
    plus_c, plus_s, minus_c, minus_s, polar_c, polar_s = tables
    left = iota((8, NB), 0) >= 3

    def columns(table, start):
        main = table[pl.ds(start + 8, F2), :]
        edge = jnp.where(left, table[pl.ds(start, 8), :], table[pl.ds(start + 97, 8), :])
        return jnp.concatenate([main, edge], axis=0)

    def two_rows(k, carry):
        n = where(k)
        for c in range(4):
            outs = []
            for h in range(2):
                t = 2 * n + h
                high = jnp.concatenate([xh[c, t], xh[c + 4, t]], axis=1)
                low = jnp.concatenate([xl[c, t], xl[c + 4, t]], axis=1)
                rhs = jnp.concatenate([high, low, high], axis=0)
                outs.append(jnp.dot(up_ref[...], rhs, preferred_element_type=F32))
            at = pl.ds(pl.multiple_of(16 * n, 16), 16)
            for g in range(12):
                rows = slice(8 * g, 8 * g + 8)
                hi, lo = halves(jnp.concatenate([outs[0][rows], outs[1][rows]], axis=0))
                vh[g, c, at, :] = hi
                vl[g, c, at, :] = lo
        for extra in range(6):
            r = jnp.minimum(6 * n + extra, ROWS - 1)
            e = times(columns(plus_c, r), columns(plus_s, r), columns(minus_c, 33 - r), columns(minus_s, 33 - r))
            e = times(*e, polar_c[pl.ds(r, 1), :], polar_s[pl.ds(r, 1), :])
            er_ref[r], ei_ref[r] = e
        return carry

    lax.fori_loop(0, count, two_rows, 0)


def up_blocks(numbers, theta_refs, z_ref, vh, vl, er_ref, ei_ref):
    keeps = [first_of_pair(m) for m in range(4)]

    def group(g, carry):
        rows = pl.ds(pl.multiple_of(8 * g, 8), 8)
        for number in numbers:
            first, last, t_first, t_last, tiles = BLOCKS[number]
            matrix = theta_refs[number]
            for c in range(4):
                part = slice(8 * t_first, 8 * t_last)
                high = vh[g, c, part, :]
                rhs = jnp.concatenate([high, vl[g, c, part, :], high], axis=0)
                v = jnp.dot(matrix[...], rhs, preferred_element_type=F32)
                for tile, start in tiles:
                    count = min(8, last - start) // 2
                    pairs = ([], [])
                    for m in range(count):
                        found = []
                        for p in (start + 2 * m, start + 2 * m + 1):
                            here = slice(8 * (p - first), 8 * (p - first) + 8)
                            e = er_ref[p + 6, rows, :], ei_ref[p + 6, rows, :]
                            found.append(times(v[here, 0:NB], v[here, NB : 2 * NB], *e))
                        for h in range(2):
                            pairs[h].append(merge(keeps[m], found[0][h], found[1][h], 64))
                    for h in range(2):
                        z_ref[tile, c + 4 * h, rows, :] = merge_tile(pairs[h], count)
        return carry

    lax.fori_loop(0, 12, group, 0, unroll=3)


def neighbours():
    theta, phi = lax.axis_index("theta"), lax.axis_index("phi")
    last = lax.axis_size("theta") - 1
    ring = lax.axis_size("phi")
    right = lax.rem(phi + 1, ring)
    left = lax.rem(phi + ring - 1, ring)
    out = []
    for dt in (-1, 0, 1):
        for df, column in ((-1, left), (0, phi), (1, right)):
            if dt == 0 and df == 0:
                continue
            has = None if dt == 0 else (theta > 0 if dt < 0 else theta < last)
            out.append((dt, df, has, (theta + dt, column)))
    return out


def guarded(has, do):
    if has is None:
        do()
    else:
        pl.when(has)(do)


def greet(around):
    barrier = pltpu.get_barrier_semaphore()
    for dt, df, has, device in around:
        def signal(device=device):
            pl.semaphore_signal(barrier, inc=1, device_id=device, device_id_type=MESH)

        guarded(has, signal)


def met(around):
    barrier = pltpu.get_barrier_semaphore()
    inside = around[0][2] & around[-1][2]

    @pl.when(inside)
    def _():
        pl.semaphore_wait(barrier, 8)

    @pl.when(jnp.logical_not(inside))
    def _():
        pl.semaphore_wait(barrier, 5)


def exchange(around, wanted, source, landing, send_sem, recv_sem):
    for n, (dt, df, has, device) in enumerate(around):
        if wanted(dt):
            copy = pltpu.make_async_remote_copy(
                src_ref=source(dt, df),
                dst_ref=landing[(-dt, -df)],
                send_sem=send_sem.at[n],
                recv_sem=recv_sem.at[7 - n],
                device_id=device,
                device_id_type=MESH,
            )
            guarded(has, copy.start)


def finish(around, wanted, source, landing, send_sem, recv_sem):
    for n, (dt, df, has, device) in enumerate(around):
        if not wanted(dt):
            continue
        copy = pltpu.make_async_remote_copy(
            src_ref=source(dt, df),
            dst_ref=landing[(dt, df)],
            send_sem=send_sem.at[n],
            recv_sem=recv_sem.at[n],
            device_id=device,
            device_id_type=MESH,
        )
        guarded(has, copy.wait)


STEP = 96


def child_setup(src_ref, kind_ref, hot_s, hot_k):
    row = lax.rem(iota((2 * NB, NB), 0), NB)
    for l in range(LIST):
        cut = slice(l * NB, l * NB + NB)
        hot_s[:, cut] = flags(row == src_ref[l : l + 1, :])
        hot_k[:, cut] = flags(row == kind_ref[l : l + 1, :])


def child_steps(low, high, x_ref, t_ref, o_ref, hot_s, hot_k, lx, lt):
    def step(g, carry):
        cut = pl.ds(2 * g, 2)
        for c in range(8):
            hi, lo = halves(x_ref[c, cut].reshape(STEP, NB))
            at = slice((2 * (c % 4) + c // 4) * STEP, (2 * (c % 4) + c // 4 + 1) * STEP)
            lx[at, 0:NB] = hi
            lx[at, NB : 2 * NB] = lo
        for c in range(2):
            hi, lo = halves(t_ref[c, cut].reshape(STEP, NB))
            lt[c * STEP : (c + 1) * STEP, 0:NB] = hi
            lt[c * STEP : (c + 1) * STEP, NB : 2 * NB] = lo
        total = [None] * 8
        for pair in range(LIST // 2):
            both = slice(pair * 2 * NB, (pair + 1) * 2 * NB)
            tt = jnp.dot(lt[...], hot_k[:, both], preferred_element_type=F32)
            for c in range(4):
                xx = jnp.dot(lx[2 * c * STEP : (2 * c + 2) * STEP, :], hot_s[:, both], preferred_element_type=F32)
                found = []
                for h in range(2):
                    one = slice(h * NB, h * NB + NB)
                    found.append(times(xx[:STEP, one], xx[STEP:, one], tt[:STEP, one], tt[STEP:, one]))
                for h in range(2):
                    value = (found[0][h] + found[1][h]).reshape(2, F1, NB)
                    if pair == 0:
                        o_ref[c + 4 * h, cut] = value
                    else:
                        o_ref[c + 4 * h, cut] += value
        return carry

    lax.fori_loop(low, high, step, 0)


def pack_right(low, high):
    return jnp.where(iota(low.shape, 1) < 3, low, pltpu.roll(high, 3, 1))


def up_source(z_ref, right_outer, right_inner):
    def source(dt, df):
        if dt == 0:
            return right_inner if df > 0 else z_ref.at[0:3, :, F2:QX, :]
        tile = 3 if dt < 0 else 4
        if df == 0:
            return z_ref.at[tile, :, 0:F2, :]
        return right_outer.at[tile - 3] if df > 0 else z_ref.at[tile, :, F2:QX, :]

    return source


def up_join(z_ref, tile, left, right):
    keep = (iota((4, 8, NB), 1) >= 1) & (iota((4, 8, NB), 1) <= 3)
    z_ref[tile, 0:4, 0:8, :] += jnp.where(keep, pltpu.roll(left, 1, 1), 0.0)
    z_ref[tile, 4:8, 0:8, :] += jnp.where(keep, pltpu.roll(left, 6, 1), 0.0)
    z_ref[tile, :, F2 - 8 : F2, :] += jnp.where(iota((8, NB), 0) >= 3, right, 0.0)


def up_join_outer(around, z_ref, landing):
    for side, has, tile in ((-1, around[0][2], 0), (1, around[-1][2], 2)):

        @pl.when(has)
        def _(side=side, tile=tile):
            z_ref[tile, :, 0:F2, :] += landing[(side, 0)][...]
            up_join(z_ref, tile, landing[(side, -1)][...], landing[(side, 1)][...])


def parent_setup(src_ref, kind_ref, hot_x, hot_t):
    row = iota((NB, NB), 0)
    for jj in range(4):
        keep = first_of_pair(jj)
        slot0, slot1 = REVERSED[2 * jj], REVERSED[2 * jj + 1]
        late_slot = jnp.where(keep, 16 * slot0, 16 * slot1)
        late = row == kind_ref[1:2, :]
        for half in range(2):
            cut = slice(half * NB, half * NB + NB)
            hot_x[jj, cut, 0:NB] = flags(row == src_ref[0:1, :] + 16 * slot0)
            hot_x[jj, cut, NB : 2 * NB] = flags(row == src_ref[0:1, :] + 16 * slot1)
            hot_x[jj, cut, 2 * NB : 3 * NB] = flags(row == src_ref[1:2, :] + late_slot)
            early = flags(row == kind_ref[0:1, :])
            hot_t[jj, 0, cut, 0:NB] = early
            hot_t[jj, 1, cut, 0:NB] = early
            hot_t[jj, 0, cut, NB : 2 * NB] = flags(late & keep)
            hot_t[jj, 1, cut, NB : 2 * NB] = flags(late & jnp.logical_not(keep))


def parent_rows(tiles, z_ref, t_ref, hot_x, hot_t, lx, lt, sums):
    lane = iota((1, NB), 1)
    halfway = [lax.rem(lane + 128 - 16 * q, 64) < 32 for q in range(2)]
    keeps = [first_of_pair(jj) for jj in range(4)]
    for tile in tiles:
        for c in range(8):
            hi, lo = halves(z_ref[tile, c, 0:F2, :])
            at = slice((2 * (c % 4) + c // 4) * F2, (2 * (c % 4) + c // 4 + 1) * F2)
            lx[tile, at, 0:NB] = hi
            lx[tile, at, NB : 2 * NB] = lo

    def quad(tile, q):
        tables = []
        for m in range(2):
            jj = 2 * q + m
            for r in range(2):
                for c in range(2):
                    hi, lo = halves(t_ref[c, jnp.minimum(8 * tile + 2 * jj + r, T2 - 1)])
                    lt[m, r, c * F2 : (c + 1) * F2, 0:NB] = hi
                    lt[m, r, c * F2 : (c + 1) * F2, NB : 2 * NB] = lo
            t0 = jnp.dot(lt[m, 0], hot_t[jj, 0], preferred_element_type=F32)
            t1 = jnp.dot(lt[m, 1], hot_t[jj, 1], preferred_element_type=F32)
            tables.append([t0[:, 0:NB], t1[:, 0:NB], t0[:, NB : 2 * NB] + t1[:, NB : 2 * NB]])
        for c in range(4):
            pairs = ([], [])
            for m in range(2):
                jj, tt = 2 * q + m, tables[m]
                xx = jnp.dot(lx[tile, 2 * c * F2 : (2 * c + 2) * F2, :], hot_x[jj], preferred_element_type=F32)
                parts = []
                for k in range(3):
                    one = slice(k * NB, k * NB + NB)
                    parts.append(times(xx[0:F2, one], xx[F2 : 2 * F2, one], tt[k][:F2], tt[k][F2:]))
                for h in range(2):
                    pairs[h].append(merge(keeps[jj], parts[0][h], parts[1][h], 64) + parts[2][h])
            for h in range(2):
                at = slice((c + 4 * h) * F2, (c + 4 * h + 1) * F2)
                sums[2 * tile + q, at, :] = merge(halfway[q], pairs[h][0], pairs[h][1], 96)

    def one_tile(k, carry):
        for q in range(2):
            quad(tiles[0] + 2 * k, q)
        return carry

    lax.fori_loop(0, len(tiles), one_tile, 0)


def parent_down(sums, theta_ref, phi_ref, w_ref, ld, rd):
    even = lax.rem(iota((1, NB), 1), 32) < 16
    for tile in range(3):
        hi, lo = halves(merge(even, sums[2 * tile], sums[2 * tile + 1], 112))
        ld[:, (3 * tile) * NB : (3 * tile + 1) * NB] = hi
        ld[:, (3 * tile + 1) * NB : (3 * tile + 2) * NB] = lo
        ld[:, (3 * tile + 2) * NB : (3 * tile + 3) * NB] = hi
    down = jnp.dot(ld[...], theta_ref[...], preferred_element_type=F32)
    for c in range(8):
        hi, lo = halves(down[c * F2 : (c + 1) * F2, :])
        cut = slice(c * 3 * NB, (c + 1) * 3 * NB)
        rd[0:F2, cut] = hi
        rd[96 : 96 + F2, cut] = lo
        rd[192 : 192 + F2, cut] = hi
    for c in range(8):
        cut = slice(c * 3 * NB, (c + 1) * 3 * NB)
        w_ref[c] = jnp.dot(phi_ref[...], rd[:, cut], preferred_element_type=F32)


def down_pack(w_ref, send_up, send_down, send_right, send_left):
    near, far = w_ref[0:4, F1:56, :], w_ref[4:8, F1:56, :]
    send_right[...] = pack_right(near, far)
    send_left[...] = jnp.where(iota(near.shape, 1) >= 5, near, pltpu.roll(far, 5, 1))
    low = iota((F1 // 2, NB), 1) < 64
    for c in range(8):
        near = w_ref[c, 0 : F1 // 2, 2 * NB : 3 * NB]
        far = pltpu.roll(w_ref[c, F1 // 2 : F1, 2 * NB : 3 * NB], 64, 1)
        send_up[c] = jnp.where(low, near, far)
        send_down[c] = jnp.where(low, far, near)


def down_source(send_up, send_down, send_right, send_left):
    def source(dt, df):
        if df == 0:
            return send_up if dt > 0 else send_down
        edge = send_right if df > 0 else send_left
        return edge.at[:, :, 0 : 2 * NB] if dt == 0 else edge.at[:, :, 2 * NB : 3 * NB]

    return source


def down_edges(wo_ref, cut, inside, left, right):
    sub = iota(left.shape, 1)
    first, last = slice(0, 8), slice(F1 - 8, F1)
    wo_ref[0:4, first, cut] += jnp.where(inside & (sub < 3), left, 0.0)
    wo_ref[4:8, first, cut] += jnp.where(inside & (sub < 3), pltpu.roll(left, 5, 1), 0.0)
    wo_ref[0:4, last, cut] += jnp.where(inside & (sub >= 5), right, 0.0)
    wo_ref[4:8, last, cut] += jnp.where(inside & (sub >= 5), pltpu.roll(right, 3, 1), 0.0)


def down_join(around, w_ref, wo_ref, landing):
    wo_ref[...] = w_ref[:, 0:F1, 0 : 2 * NB]
    all_lanes = iota((4, 8, 2 * NB), 2) >= 0
    down_edges(wo_ref, slice(0, 2 * NB), all_lanes, landing[(0, -1)][...], landing[(0, 1)][...])
    half = F1 // 2
    lane, lane8 = iota((half, NB), 1), iota((4, 8, NB), 2)

    @pl.when(around[0][2])
    def _():
        cut = slice(0, NB)
        for c in range(8):
            got = landing[(-1, 0)][c]
            wo_ref[c, 0:half, cut] += jnp.where(lane < 48, got, 0.0)
            wo_ref[c, half:F1, cut] += jnp.where(lane < 48, pltpu.roll(got, 64, 1), 0.0)
        down_edges(wo_ref, cut, lane8 < 48, landing[(-1, -1)][...], landing[(-1, 1)][...])

    @pl.when(around[-1][2])
    def _():
        cut = slice(NB, 2 * NB)
        keep = (lane >= 16) & (lane < 64)
        for c in range(8):
            got = landing[(1, 0)][c]
            wo_ref[c, 0:half, cut] += jnp.where(keep, pltpu.roll(got, 64, 1), 0.0)
            wo_ref[c, half:F1, cut] += jnp.where(keep, got, 0.0)
        left, right = pltpu.roll(landing[(1, -1)][...], 64, 2), pltpu.roll(landing[(1, 1)][...], 64, 2)
        down_edges(wo_ref, cut, (lane8 >= 16) & (lane8 < 64), left, right)


EARLY = 4


def main_kernel(
    index_ref, table_ref, x_far, tc_far, tp_far, theta_far, up_ref, ta_ref, tb_ref, tc2_ref, td_ref, phi_ref, wo_ref, local_far, *scratch
):
    up_land, down_land, up_sems, down_sems = scratch[0:8], scratch[8:16], scratch[16:18], scratch[18:20]
    z_ref, lhs, order, xh, xl, vh, vl, er_ref, ei_ref = scratch[20:29]
    tables = views(table_ref, UP_ROWS)
    hot_s, hot_k, lx, lt = scratch[29:33]
    hot_x, hot_t, plx, plt, sums, ld, rd, w_ref = scratch[33:41]
    x_ref, tc_ref, tp_ref, theta_ref, local_ref, send_up, send_down, load_sem, store_sem = scratch[41:50]
    right_outer, right_inner, send_right, send_left = scratch[50:54]
    loads = [
        pltpu.make_async_copy(far, near, load_sem.at[n])
        for n, (far, near) in enumerate(
            ((x_far, x_ref), (tc_far, tc_ref), (tp_far, tp_ref), (theta_far, theta_ref))
        )
    ]
    stores = [
        pltpu.make_async_copy(local_ref.at[:, rows], local_far.at[:, rows], store_sem.at[n])
        for n, rows in enumerate((slice(0, 2 * EARLY), slice(2 * EARLY, T1)))
    ]
    for load in loads:
        load.start()
    keys = [(-1, 0), (1, 0), (0, -1), (0, 1), (-1, -1), (-1, 1), (1, -1), (1, 1)]
    up_landing, down_landing = dict(zip(keys, up_land)), dict(zip(keys, down_land))
    around = neighbours()
    greet(around)
    up_turn(index_ref[0:NB, :], loads[0], x_ref, lhs, order, xh, xl)
    column_refs = (up_ref, xh, xl, vh, vl, er_ref, ei_ref, tables)
    up_columns(4, lambda k: k + 2 * (k // 2), *column_refs)
    shared = ((ta_ref, tb_ref, tc2_ref, td_ref), z_ref, vh, vl, er_ref, ei_ref)
    up_blocks((0, 1), *shared)
    met(around)
    for n in range(2):
        right_outer[n] = pack_right(z_ref[3 + n, 0:4, F2:QX, :], z_ref[3 + n, 4:8, F2:QX, :])
    source = up_source(z_ref, right_outer, right_inner)
    exchange(around, lambda dt: dt != 0, source, up_landing, *up_sems)
    up_columns(2, lambda k: k + 2, *column_refs)
    up_blocks((2, 3), *shared)
    for n in range(3):
        right_inner[n] = pack_right(z_ref[n, 0:4, F2:QX, :], z_ref[n, 4:8, F2:QX, :])
    exchange(around, lambda dt: dt == 0, source, up_landing, *up_sems)
    child_setup(index_ref.at[NB + 8 : NB + 24], index_ref.at[NB + 24 : NB + 40], hot_s, hot_k)
    children = (x_ref, tc_ref, local_ref, hot_s, hot_k, lx, lt)
    rd[...] = jnp.zeros_like(rd)
    parent_setup(index_ref.at[NB + 20 : NB + 22], index_ref.at[NB + 36 : NB + 38], hot_x, hot_t)
    loads[1].wait()
    child_steps(0, EARLY, *children)
    stores[0].start()
    finish(around, lambda dt: dt == 0, source, up_landing, *up_sems)
    for tile in range(3):
        up_join(z_ref, tile, up_landing[(0, -1)][tile], up_landing[(0, 1)][tile])
    loads[2].wait()
    parent = (z_ref, tp_ref, hot_x, hot_t, plx, plt, sums)
    parent_rows((1,), *parent)
    finish(around, lambda dt: dt != 0, source, up_landing, *up_sems)
    up_join_outer(around, z_ref, up_landing)
    parent_rows((0, 2), *parent)
    loads[3].wait()
    parent_down(sums, theta_ref, phi_ref, w_ref, ld, rd)
    down_pack(w_ref, send_up, send_down, send_right, send_left)
    source = down_source(send_up, send_down, send_right, send_left)
    exchange(around, lambda dt: True, source, down_landing, *down_sems)
    child_steps(EARLY, T1 // 2, *children)
    stores[1].start()
    finish(around, lambda dt: True, source, down_landing, *down_sems)
    down_join(around, w_ref, wo_ref, down_landing)
    for store in stores:
        store.wait()


FINAL = 2


def final_kernel(slot_ref, table_ref, w_ref, local_far, o_far, lw, spread, local_ref, o_ref, load_sem, store_sem):
    parts = [slice(n * FINAL, n * FINAL + FINAL) for n in range(T1 // FINAL)]
    loads = [
        pltpu.make_async_copy(local_far.at[:, rows], local_ref.at[:, rows], load_sem.at[n])
        for n, rows in enumerate(parts)
    ]
    stores = [
        pltpu.make_async_copy(o_ref.at[:, rows], o_far.at[:, rows], store_sem.at[n])
        for n, rows in enumerate(parts)
    ]
    for load in loads:
        load.start()
    plus_c, plus_s, minus_c, minus_s, polar_c, polar_s = views(table_ref, DOWN_ROWS)

    row = iota((NB, NB), 0)
    parent = lax.rem(jnp.broadcast_to(slot_ref[...], (NB, NB)), 16)
    for j in range(8):
        block = flags(row == parent + 16 * j)
        spread[j, 0:NB, :] = block
        spread[j, NB : 2 * NB, :] = block
    for tile in range(2):
        for c in range(8):
            hi, lo = halves(w_ref[c, :, tile * NB : (tile + 1) * NB])
            lw[tile, c * F1 : (c + 1) * F1, 0:NB] = hi
            lw[tile, c * F1 : (c + 1) * F1, NB : 2 * NB] = lo

    def one_row(t):
        wide = jnp.dot(lw[t // 8], spread[t % 8], preferred_element_type=F32)
        er, ei = times(
            plus_c[pl.ds(t, F1), :],
            plus_s[pl.ds(t, F1), :],
            minus_c[pl.ds(11 - t, F1), :],
            minus_s[pl.ds(11 - t, F1), :],
        )
        er, ei = times(er, ei, polar_c[pl.ds(t, 1), :], polar_s[pl.ds(t, 1), :])
        for c in range(4):
            u, v = wide[c * F1 : (c + 1) * F1], wide[(c + 4) * F1 : (c + 5) * F1]
            re, im = times(u, v, er, -ei)
            o_ref[c, t] = re + local_ref[c, t]
            o_ref[c + 4, t] = im + local_ref[c + 4, t]

    for n in range(T1 // FINAL):
        loads[n].wait()
        for t in range(n * FINAL, n * FINAL + FINAL):
            one_row(t)
        stores[n].start()
    for store in stores:
        store.wait()


def shape(*dims):
    return jax.ShapeDtypeStruct(dims, F32)


def landing_scratch(outer, left, right, corner_left, corner_right):
    return [pltpu.VMEM(dims, F32) for dims in [outer] * 2 + [left, right] + [corner_left, corner_right] * 2]


def per_device(child_out, child_slot, sources_child, kinds_child, table_child, sources_parent, kinds_parent, table_parent):
    slot_row = child_slot.reshape(1, NB)
    params = dict(vmem_limit_bytes=60 * 1024 * 1024)
    index, up_table, down_table = pl.pallas_call(
        index_kernel,
        out_shape=(
            jax.ShapeDtypeStruct((INDEX_ROWS, NB), jnp.int32),
            shape(table_rows(UP_ROWS)[1], NB),
            shape(table_rows(DOWN_ROWS)[1], NB),
        ),
        in_specs=[VM] * 5,
        out_specs=(VM, VM, VM),
        scratch_shapes=[pltpu.VMEM((NB, NB), jnp.int32)],
        name="index",
    )(slot_row, sources_child.T, kinds_child.T, sources_parent, kinds_parent)

    wo, local = pl.pallas_call(
        main_kernel,
        out_shape=(shape(8, F1, 2 * NB), shape(8, T1, F1, NB)),
        in_specs=[VM] * 2 + [ANY] * 4 + [VM] * 6,
        out_specs=(VM, ANY),
        scratch_shapes=landing_scratch((8, F2, NB), (3, 4, 8, NB), (3, 8, 8, NB), (4, 8, NB), (8, 8, NB))
        + landing_scratch((8, F1 // 2, NB), (4, 8, 2 * NB), (4, 8, 2 * NB), (4, 8, NB), (4, 8, NB))
        + [pltpu.SemaphoreType.DMA((8,))] * 4
        + [
            pltpu.VMEM((5, 8, QX, NB), F32),
            pltpu.VMEM((T1 * F1, 2 * NB), BF16),
            pltpu.VMEM((2 * NB, 2 * NB), BF16),
            pltpu.VMEM((8, T1, F1, NB), BF16),
            pltpu.VMEM((8, T1, F1, NB), BF16),
            pltpu.VMEM((12, 4, 8 * T1, 2 * NB), BF16),
            pltpu.VMEM((12, 4, 8 * T1, 2 * NB), BF16),
            pltpu.VMEM((ROWS, QX, NB), F32),
            pltpu.VMEM((ROWS, QX, NB), F32),
        ]
        + [pltpu.VMEM((2 * NB, LIST * NB), BF16)] * 2
        + [pltpu.VMEM((8 * STEP, 2 * NB), BF16), pltpu.VMEM((2 * STEP, 2 * NB), BF16)]
        + [
            pltpu.VMEM((4, 2 * NB, 3 * NB), BF16),
            pltpu.VMEM((4, 2, 2 * NB, 2 * NB), BF16),
            pltpu.VMEM((3, 8 * F2, 2 * NB), BF16),
            pltpu.VMEM((2, 2, 2 * F2, 2 * NB), BF16),
            pltpu.VMEM((6, 8 * F2, NB), F32),
            pltpu.VMEM((8 * F2, 9 * NB), BF16),
            pltpu.VMEM((288, 8 * 3 * NB), BF16),
            pltpu.VMEM((8, 56, 3 * NB), F32),
            pltpu.VMEM((8, T1, F1, NB), F32),
            pltpu.VMEM((2, T1, F1, NB), F32),
            pltpu.VMEM((2, T2, F2, NB), F32),
            pltpu.VMEM((9 * NB, 3 * NB), BF16),
            pltpu.VMEM((8, T1, F1, NB), F32),
            pltpu.VMEM((8, F1 // 2, NB), F32),
            pltpu.VMEM((8, F1 // 2, NB), F32),
            pltpu.SemaphoreType.DMA((4,)),
            pltpu.SemaphoreType.DMA((2,)),
            pltpu.VMEM((2, 4, 8, NB), F32),
            pltpu.VMEM((3, 4, 8, NB), F32),
            pltpu.VMEM((4, 8, 3 * NB), F32),
            pltpu.VMEM((4, 8, 3 * NB), F32),
        ],
        compiler_params=pltpu.CompilerParams(collective_id=0, has_side_effects=True, **params),
        name="main",
    )(
        index,
        up_table,
        child_out,
        table_child,
        table_parent,
        jnp.asarray(theta_down()),
        jnp.asarray(phi_up()),
        *[jnp.asarray(theta_up(*block[:4])) for block in BLOCKS],
        jnp.asarray(phi_down()),
    )

    return pl.pallas_call(
        final_kernel,
        out_shape=shape(8, T1, F1, NB),
        in_specs=[VM, VM, VM, ANY],
        out_specs=ANY,
        scratch_shapes=[
            pltpu.VMEM((2, 8 * F1, 2 * NB), BF16),
            pltpu.VMEM((8, 2 * NB, NB), BF16),
            pltpu.VMEM((8, T1, F1, NB), F32),
            pltpu.VMEM((8, T1, F1, NB), F32),
            pltpu.SemaphoreType.DMA((T1 // FINAL,)),
            pltpu.SemaphoreType.DMA((T1 // FINAL,)),
        ],
        compiler_params=pltpu.CompilerParams(**params),
        name="final",
    )(slot_row, down_table, wo, local)


def solution(mesh):
    block = P(None, "theta", "phi", None)
    return jax.shard_map(
        per_device,
        mesh=mesh,
        in_specs=(block, P(), P(), P(), block, P(), P(), block),
        out_specs=block,
        check_vma=False,
    )
```
